128 devices in a mesh: section: 8 (over y, core), tp: 16 (over x, z).
Axes of the slice: x: 4, y: 4, z: 4, core: 2. Of those that a mesh axis runs over, the one named last changes fastest.
Arguments:
- stream_in: bfloat16 [512, 8192], P(None, 'tp')
- layer_delta: bfloat16 [8, 512, 8192], P('section', None, 'tp')
- norm_gain: float32 [8192], P('tp'), may hold values from 0.25 to 1.75
- out_embed: bfloat16 [8192, 16384], P(None, 'tp')
- exit_blocks: int32 [8, 4], P('section'), may hold values from 0 to 3
- exit_counts: int32 [8], P('section'), may hold values from 1 to 4, 16 in all
- targets: int32 [512], replicated, may hold values from 0 to 16383
Outputs:
- exit_loss: float32 [8, 4, 128], P('section')
The draws below stay inside these ranges and needn't reach their ends.
Inputs may be any that keep to these rules, and one draw needn't show every extreme that they name: `exit_counts`: each section scores at least one block, the counts of all sections sum to 2 times the number of sections, and some section scores exactly 4. `exit_blocks`: block numbers of the micro-batch's 128-row blocks; only a section's first exit_counts entries are used.
All inputs are finite; a program needn't handle non-finite values.
Results may differ from the reference program's by a relative error of at most 0.02.
Values may be sent and summed in bfloat16 or wider, within the bound.
A program may use at most 128 MiB of HBM per device.

```python
import math
import jax
import jax.numpy as jnp
import numpy as np
from jax import lax

D = 8192
VOC = 16384
R = 512
BLK = 128
MAXB = 4
MEANB = 2
N_SECTION = 8


def column_profile(width):
    position = jnp.arange(width, dtype=jnp.float32) / jnp.float32(max(width - 1, 1))
    return jnp.exp(position * jnp.log(jnp.float32(3.16)))


def rough_values(key, shape):
    return jnp.clip(jax.random.normal(key, shape, jnp.float32), -4.0, 4.0)


def draw_stream_in(key, part):
    values = rough_values(jax.random.fold_in(key, 11), (R, D))
    return (values * column_profile(D)[None, :]).astype(jnp.bfloat16)


def draw_layer_delta(key, part):
    values = rough_values(jax.random.fold_in(key, 23), (N_SECTION, R, D))
    return (0.5 * values * column_profile(D)[None, None, :]).astype(jnp.bfloat16)


def draw_out_embed(key, part):
    base = jax.random.normal(key, (D, VOC), jnp.float32) * (3.0 / D ** 0.5)
    return base.astype(jnp.bfloat16)


def plant(array, stream_key, least, high):
    index_at = [jax.random.randint(jax.random.fold_in(stream_key, axis), (), 0, length) for axis, length in enumerate(array.shape)]
    widest = array.shape.index(max(array.shape))
    beside = index_at[:widest] + [(index_at[widest] + 1) % array.shape[widest]] + index_at[widest + 1:]
    return array.at[tuple(index_at)].set(least).at[tuple(beside)].set(high)


def cumulative_ranks(number_of, slope):
    loads = [(1 << 20) // math.isqrt(grade ** slope) + 1 for grade in range(1, number_of + 1)]
    scale = 1 + sum(loads) // (1 << 30)
    return np.cumsum(np.array([max(1, weight // scale) for weight in loads]))


def ranked_ids(own_key, dims, count, skew):
    table = cumulative_ranks(count, skew)
    ticket = jax.random.randint(jax.random.fold_in(own_key, 1), dims, 0, int(table[count - 1]))
    grade = jnp.searchsorted(jnp.asarray(table, jnp.int32), ticket, side="right")
    return jax.random.permutation(jax.random.fold_in(own_key, 2), count)[grade].astype(jnp.int32)


def split_up(count, total, reach, skew):
    loads = [(1 << 20) // math.isqrt(rank ** skew) + 1 for rank in range(2, count + 1)]
    spare, given = total - reach - (count - 1), [1] * (count - 1)
    while spare > 0:
        free = [i for i in range(count - 1) if given[i] < reach]
        whole, remaining = sum([loads[i] for i in free]), spare
        for i in free:
            addition = min(reach - given[i], max(1, remaining * loads[i] // whole), spare)
            given[i] = given[i] + addition
            spare = spare - addition
    return np.array([reach] + given)


def uneven_parts(stream_key, amount, total, most, slope):
    if amount == 2:
        one = jax.random.randint(stream_key, (), max(1, total - most), min(most, total - 1) + 1)
        return jnp.stack([one, total - one])
    sizes = jnp.asarray(split_up(amount, total, most, slope), jnp.int32)
    twos = (amount - 1) // 2
    giver, taker = sizes[1:1 + 2 * twos:2], sizes[2:2 + 2 * twos:2]
    slack = jnp.minimum(giver - 1, most - taker)
    moved = jax.random.randint(jax.random.fold_in(stream_key, 1), (twos,), 0, 1 << 20) % (slack + 1)
    sizes = sizes.at[1:1 + 2 * twos:2].set(giver - moved).at[2:2 + 2 * twos:2].set(taker + moved)
    return sizes[jax.random.permutation(jax.random.fold_in(stream_key, 2), amount)]


def setup_inputs(seed: int = 0) -> dict:
    key_list = jax.random.split(jax.random.key(seed), 8)
    return {
        "stream_in": draw_stream_in(jax.random.fold_in(key_list[7], 71), 0),
        "layer_delta": draw_layer_delta(jax.random.fold_in(key_list[7], 71), 0),
        "norm_gain": jnp.clip(1.0 + 0.15 * jax.random.normal(key_list[2], (D,), jnp.float32), 0.25, 1.75),
        "out_embed": draw_out_embed(jax.random.fold_in(key_list[7], 71), 0),
        "exit_blocks": plant(jax.random.randint(key_list[4], (N_SECTION, MAXB), 0, R // BLK), jax.random.fold_in(key_list[4], 1), 0, (R // BLK) - 1).astype(jnp.int32),
        "exit_counts": uneven_parts(key_list[5], N_SECTION, MEANB * N_SECTION, MAXB, 2).astype(jnp.int32),
        "targets": plant(ranked_ids(key_list[6], (R,), VOC, 2), jax.random.fold_in(key_list[6], 3), 0, VOC - 1).astype(jnp.int32),
    }


EPS = 1e-05

def normed_rows(rows, norm_gain):
    scale = lax.rsqrt(lax.optimization_barrier(jnp.mean(rows * rows, axis=1)) + EPS)
    return (rows * scale[:, None] * norm_gain[None, :]).astype(jnp.bfloat16)

def row_loss(logit_exit, logit_teach, target_rows):
    peak_exit = lax.optimization_barrier(jnp.max(logit_exit, axis=1))
    total_exit = lax.optimization_barrier(jnp.sum(jnp.exp(logit_exit - peak_exit[:, None]), axis=1))
    peak_teach = lax.optimization_barrier(jnp.max(logit_teach, axis=1))
    weight_teach = jnp.exp(logit_teach - peak_teach[:, None])
    total_teach = lax.optimization_barrier(jnp.sum(weight_teach, axis=1))
    cross = lax.optimization_barrier(jnp.sum(weight_teach * (logit_teach - logit_exit), axis=1))
    picked = jnp.take_along_axis(logit_exit, target_rows[:, None], axis=1)[:, 0]
    log_exit = jnp.log(total_exit) + peak_exit
    log_teach = jnp.log(total_teach) + peak_teach
    return 2.0 * log_exit - picked + cross / total_teach - log_teach

def reference(stream_in, layer_delta, norm_gain, out_embed, exit_blocks, exit_counts, targets):
    stream = stream_in.astype(jnp.float32)
    deltas = layer_delta.astype(jnp.float32)
    final = stream + lax.optimization_barrier(jnp.sum(deltas, axis=0))
    teach_all = jnp.dot(normed_rows(final, norm_gain), out_embed, preferred_element_type=jnp.float32)
    counts = exit_counts.astype(jnp.int32)
    offsets = (jnp.cumsum(counts) - counts).astype(jnp.int32)
    section_ids = jnp.arange(N_SECTION, dtype=jnp.int32)

    def one_pair(pair):
        owner = (jnp.sum((offsets <= pair).astype(jnp.int32)) - 1).astype(jnp.int32)
        slot = (pair - offsets[owner]).astype(jnp.int32)
        start = (exit_blocks[owner, slot] * BLK).astype(jnp.int32)
        rows = lax.dynamic_slice_in_dim(deltas, start, BLK, 1)
        upto = (section_ids <= owner).astype(jnp.float32)
        exit_rows = lax.dynamic_slice_in_dim(stream, start, BLK, 0) + lax.optimization_barrier(jnp.sum(upto[:, None, None] * rows, axis=0))
        logit_exit = jnp.dot(normed_rows(exit_rows, norm_gain), out_embed, preferred_element_type=jnp.float32)
        logit_teach = lax.dynamic_slice_in_dim(teach_all, start, BLK, 0)
        target_rows = lax.dynamic_slice_in_dim(targets, start, BLK, 0)
        return row_loss(logit_exit, logit_teach, target_rows)
    losses = lax.map(one_pair, jnp.arange(MEANB * N_SECTION, dtype=jnp.int32))
    slots = jnp.arange(MAXB, dtype=jnp.int32)
    index = jnp.minimum(offsets[:, None] + slots[None, :], MEANB * N_SECTION - 1).astype(jnp.int32)
    picked = losses[index]
    keep = slots[None, :] < counts[:, None]
    return jnp.where(keep[:, :, None], picked, jnp.float32(0.0))
```

```python
import functools
import itertools

import jax
import jax.numpy as jnp
from jax import lax
from jax.experimental import pallas as pl
from jax.experimental.pallas import tpu as pltpu
from jax.sharding import PartitionSpec as P

BLK = 128
MAXB = 4
EPS = 1e-05
NS = 8
TX = 4
TZ = 4
NT = TX * TZ
SUB = BLK // NS
NPAIR = 2 * NS
NB = 4
NG = NPAIR - 1 + NB
ROWS = NG * SUB
LANE = 128
NC = 4
WIDTH = LANE * NC * NT
VPART = 1024
NTILE = 512
DOWN = 2.0 ** -58
UP = 2.0 ** 58
F32 = jnp.float32
MESH = pl.DeviceIdType.MESH
ORDER = (0, 2, 1, 3)


def long_sign(c):
    return 1 if c % 2 == 0 else -1


def rel_of(c, a, b):
    dx, dz = (a, b) if c < NC // 2 else (b, a)
    return (dx % TX) * TZ + dz % TZ


def step_of(c, axis, sign):
    along_x = (axis == 0) == (c < NC // 2)
    return (sign, 0) if along_x else (0, sign)


def forwards(c, a, b):
    go = long_sign(c)
    if (a, b) == (0, 0):
        return [(0, go), (0, -go), (1, go), (1, -go)]
    if b == 0:
        out = [(0, go)] if a == -go else []
        return out + [(1, go), (1, -go)]
    return [(1, go)] if b == -go else []


def wrap(v):
    v = v % 4
    return v - 4 if v == 3 else v


def events():
    out = []
    for dist in range(1, 5):
        for c in ORDER:
            go = long_sign(c)
            places = [(2, 0), (-go, 0), (go, 0), (2, -go), (2, go), (-go, -go), (go, -go), (0, -go)]
            places += [(-go, go), (go, go), (0, go), (0, 2), (-go, 2), (go, 2), (2, 2)]
            out += [(c, a, b) for a, b in places if abs(a) + abs(b) == dist]
    return out


def plan():
    ready = {(0, 0): 2, (0, 1): 2}
    queue = [(0, 0), (0, 1)]
    steps = []
    for c, a, b in events():
        steps.append(("wait", c, a, b))
        key = (rel_of(c, a, b), c // 2)
        ready[key] = ready.get(key, 0) + 1
        if ready[key] == 2:
            queue.append(key)
        if queue:
            steps.append(("dot",) + queue.pop(0))
    return steps + [("dot",) + key for key in queue]


STEPS = plan()
FIRST_USE = list(dict.fromkeys(s[1] for s in STEPS if s[0] == "dot"))


def merge(parts):
    peak_e = functools.reduce(jnp.maximum, [p[0:1] for p in parts])
    peak_t = functools.reduce(jnp.maximum, [p[2:3] for p in parts])
    sum_e = sum_t = cross = picked = 0.0
    for p in parts:
        fe = jnp.exp(p[0:1] - peak_e)
        ft = jnp.exp(p[2:3] - peak_t)
        sum_e = sum_e + p[1:2] * fe
        sum_t = sum_t + p[3:4] * ft
        cross = cross + p[4:5] * ft
        picked = picked + p[5:6]
    return peak_e, sum_e, peak_t, sum_t, cross, picked


def kernel(
    eb_hbm, ec_hbm, gain_hbm, tgt_hbm, stream_hbm, delta_hbm, w_hbm, out_ref,
    eb_s, ec_s, meta_s, own_s, blk_s, grp_s,
    gain_v, tgt_v, stream_v, meta_src, meta_v, abuf, hid, sq, gath, wv, acc,
    ss_x, ss_z, scale_v, prob_v, tstat, tcol, pst, st_x, st_z, loss_y, tot_v,
    loc_sem, w_sem, meta_send, meta_recv, a_send, a_recv, g_send, g_recv, ex_send, ex_recv, y_send, y_recv,
):
    sec = lax.axis_index("section")
    tp = lax.axis_index("tp")
    px, pz = tp // TZ, tp % TZ

    def plane(dx, dz):
        return (sec, ((px + dx) % TX) * TZ + (pz + dz) % TZ)

    sec_peers = [((sec + k) % NS, tp) for k in range(1, NS)]
    x_peers = [plane(k, 0) for k in range(1, TX)]
    z_peers = [plane(0, k) for k in range(1, TZ)]
    everyone = sec_peers + x_peers + z_peers

    barrier = pltpu.get_barrier_semaphore()
    for peer in everyone:
        pl.semaphore_signal(barrier, inc=1, device_id=peer, device_id_type=MESH)

    local = [
        pltpu.make_async_copy(eb_hbm, eb_s, loc_sem.at[0]),
        pltpu.make_async_copy(ec_hbm, ec_s, loc_sem.at[1]),
        pltpu.make_async_copy(stream_hbm.at[:, sec], stream_v, loc_sem.at[2]),
        pltpu.make_async_copy(gain_hbm, gain_v, loc_sem.at[3]),
        pltpu.make_async_copy(tgt_hbm, tgt_v, loc_sem.at[4]),
    ]
    own_delta = [
        pltpu.make_async_copy(
            delta_hbm.at[:, sec, :, pl.ds(c * LANE, LANE)], abuf.at[c, sec], loc_sem.at[5 + c]
        )
        for c in range(NC)
    ]
    for copy in local + own_delta:
        copy.start()

    local[0].wait()
    local[1].wait()
    lane1 = lax.broadcasted_iota(jnp.int32, (1, LANE), 1)
    info = jnp.where(lane1 == MAXB, ec_s[0], 0)
    for k in range(MAXB):
        info = jnp.where(lane1 == k, eb_s[0, k], info)
    meta_src[...] = info
    meta_v[pl.ds(sec, 1), :, :] = info[None]

    pl.semaphore_wait(barrier, len(everyone))

    sends = []

    def send(src, dst, send_sem, recv_sem, peer):
        copy = pltpu.make_async_remote_copy(
            src_ref=src, dst_ref=dst, send_sem=send_sem, recv_sem=recv_sem,
            device_id=peer, device_id_type=MESH,
        )
        copy.start()
        sends.append(copy)

    def arrived(dst, recv_sem, any_sem):
        pltpu.make_async_remote_copy(
            src_ref=dst, dst_ref=dst, send_sem=any_sem, recv_sem=recv_sem,
            device_id=x_peers[0], device_id_type=MESH,
        ).wait_recv()

    for k, peer in enumerate(sec_peers):
        send(meta_src, meta_v.at[sec], meta_send.at[k], meta_recv.at[sec], peer)
    for c in ORDER:
        for k, peer in enumerate(sec_peers):
            send(
                delta_hbm.at[:, peer[0], :, pl.ds(c * LANE, LANE)], abuf.at[c, sec],
                a_send.at[c, k], a_recv.at[c, sec], peer,
            )

    w_copies = {}
    for i, rel in enumerate(FIRST_USE):
        src_tp = ((px + rel // TZ) % TX) * TZ + (pz + rel % TZ) % TZ
        w_copies[rel] = pltpu.make_async_copy(w_hbm.at[src_tp], wv.at[rel], w_sem.at[i])
        w_copies[rel].start()

    for peer in sec_peers:
        arrived(meta_v.at[peer[0]], meta_recv.at[peer[0]], meta_send.at[0])
    to_smem = pltpu.make_async_copy(meta_v, meta_s, loc_sem.at[9])
    to_smem.start()
    to_smem.wait()
    counts = [meta_s[u, 0, MAXB] for u in range(NS)]
    offs = [jnp.int32(0)]
    for u in range(NS - 1):
        offs.append(offs[-1] + counts[u])
    for j in range(NPAIR):
        owner = jnp.int32(0)
        base = jnp.int32(0)
        for u in range(1, NS):
            owner = jnp.where(offs[u] <= j, u, owner)
            base = jnp.where(offs[u] <= j, offs[u], base)
        block = meta_s[owner, 0, j - base]
        own_s[j] = owner
        blk_s[j] = block
        grp_s[j] = j if j < NPAIR - 1 else NPAIR - 1 + block

    local[2].wait()
    local[3].wait()
    local[4].wait()
    lane_r = lax.broadcasted_iota(jnp.int32, (SUB, LANE), 1)
    sub_r = lax.broadcasted_iota(jnp.int32, (SUB, LANE), 0)
    mine = lane_r == sec * SUB + sub_r
    for b in range(NB):
        row = jnp.broadcast_to(tgt_v[b : b + 1, :].astype(F32), (SUB, LANE))
        col = jnp.sum(jnp.where(mine, row, 0.0), axis=1, keepdims=True)
        tcol[b] = jnp.broadcast_to(col, (SUB, LANE)) - (tp * VPART).astype(F32)

    hop = itertools.count()

    def pass_on(c, a, b):
        rel = rel_of(c, a, b)
        for axis, sign in forwards(c, a, b):
            aa, bb = (wrap(a - sign), b) if axis == 0 else (a, wrap(b - sign))
            there = rel_of(c, aa, bb)
            send(
                gath.at[rel, c], gath.at[there, c],
                g_send.at[next(hop)], g_recv.at[there, c],
                plane(*step_of(c, axis, sign)),
            )

    for n, c in enumerate(ORDER):
        own_delta[c].wait()
        for peer in sec_peers:
            arrived(abuf.at[c, peer[0]], a_recv.at[c, peer[0]], a_send.at[0, 0])
        lanes = pl.ds(c * LANE, LANE)
        state = stream_v[:, :, lanes].astype(F32)
        for u in range(NS):
            state = state + abuf[c, u].astype(F32)
            hid[u] = state
        gain = gain_v[c : c + 1, :] * DOWN

        def put(g, rows, c=c, n=n, gain=gain):
            sq[g] = rows * rows if n == 0 else sq[g] + rows * rows
            gath[0, c, pl.ds(g * SUB, SUB), :] = (rows * gain).astype(jnp.bfloat16)

        for j in range(NPAIR - 1):
            put(j, hid[own_s[j], blk_s[j]])
        for b in range(NB):
            put(NPAIR - 1 + b, hid[NS - 1, b])
        pass_on(c, 0, 0)

    for g in range(NG, 24):
        sq[g] = jnp.zeros((SUB, LANE), F32)
    sums = []
    for q in range(3):
        part = sq[pl.ds(q * 8, 8)].reshape(LANE, LANE)
        sums.append(jnp.sum(part.T, axis=0, keepdims=True))
    ss_x[px] = jnp.concatenate(sums + [jnp.zeros((5, LANE), F32)], axis=0)

    def share(buf, place, peers, stage):
        for k, peer in enumerate(peers):
            send(buf.at[place], buf.at[place], ex_send.at[stage, k], ex_recv.at[stage, place], peer)

    def collect(buf, place, stage):
        for k in range(1, 4):
            there = (place + k) % 4
            arrived(buf.at[there], ex_recv.at[stage, there], ex_send.at[stage, 0])

    share(ss_x, px, x_peers, 0)

    seen = set()
    waits = 0
    for step in STEPS:
        if step[0] == "wait":
            _, c, a, b = step
            rel = rel_of(c, a, b)
            arrived(gath.at[rel, c], g_recv.at[rel, c], g_send.at[0])
            pass_on(c, a, b)
            waits += 1
            if waits == 12:
                collect(ss_x, px, 0)
                ss_z[pz] = ss_x[0] + ss_x[1] + ss_x[2] + ss_x[3]
                share(ss_z, pz, z_peers, 1)
            if waits == 36:
                collect(ss_z, pz, 1)
                total = ss_z[0] + ss_z[1] + ss_z[2] + ss_z[3]
                scale = lax.rsqrt(total / WIDTH + EPS) * UP
                for q in range(3):
                    wide = jnp.broadcast_to(scale[q : q + 1, :], (LANE, LANE)).T
                    scale_v[pl.ds(q * 8, 8)] = wide.reshape(8, SUB, LANE)
        else:
            _, rel, half = step
            if rel not in seen:
                w_copies[rel].wait()
            first = not seen
            seen.add(rel)

            def tile(n, carry, rel=rel, half=half, first=first):
                cols = pl.ds(pl.multiple_of(n * NTILE, NTILE), NTILE)
                lhs = jnp.concatenate([gath[rel, 2 * half], gath[rel, 2 * half + 1]], axis=1)
                rhs = wv[rel, pl.ds(half * 2 * LANE, 2 * LANE), cols]
                part = jnp.dot(lhs, rhs, preferred_element_type=F32).reshape(NG, SUB, NTILE)
                acc[:, :, cols] = part if first else acc[:, :, cols] + part
                return carry

            lax.fori_loop(0, VPART // NTILE, tile, 0)

    def wide8(v):
        return jnp.concatenate([v] * (VPART // LANE), axis=1)

    def teach(b, carry):
        logit = acc[NPAIR - 1 + b] * wide8(scale_v[NPAIR - 1 + b])
        peak = jnp.max(logit, axis=1, keepdims=True)
        weight = jnp.exp(logit - peak)
        prob_v[b] = weight
        total = jnp.sum(weight, axis=1, keepdims=True)
        tstat[b] = jnp.where(lane_r == 2, peak, jnp.where(lane_r == 3, total, 0.0))
        return carry

    lax.fori_loop(0, NB, teach, 0)
    column = lax.broadcasted_iota(jnp.int32, (SUB, VPART), 1).astype(F32)

    def leave(j, carry):
        block = blk_s[j]
        group = grp_s[j]
        exit_logit = acc[group] * wide8(scale_v[group])
        teach_logit = acc[NPAIR - 1 + block] * wide8(scale_v[NPAIR - 1 + block])
        weight = prob_v[block]
        peak = jnp.max(exit_logit, axis=1, keepdims=True)
        total = jnp.sum(jnp.exp(exit_logit - peak), axis=1, keepdims=True)
        cross = jnp.sum(weight * (teach_logit - exit_logit), axis=1, keepdims=True)
        hit = wide8(tcol[block]) == column
        picked = jnp.sum(jnp.where(hit, exit_logit, 0.0), axis=1, keepdims=True)
        out = tstat[block]
        for k, v in ((0, peak), (1, total), (4, cross), (5, picked)):
            out = jnp.where(lane_r == k, v, out)
        pst[j] = out
        return carry

    lax.fori_loop(0, NPAIR, leave, 0)
    stats = [pst[pl.ds(q * 8, 8)].reshape(LANE, LANE).T[0:8, :] for q in range(2)]
    st_x[px] = jnp.concatenate(stats, axis=1)
    share(st_x, px, x_peers, 2)
    collect(st_x, px, 2)
    joined = merge([st_x[i] for i in range(TX)])
    st_z[pz] = jnp.concatenate(list(joined) + [jnp.zeros((2, NPAIR * SUB), F32)], axis=0)
    share(st_z, pz, z_peers, 3)
    collect(st_z, pz, 3)
    peak_e, sum_e, peak_t, sum_t, cross, picked = merge([st_z[i] for i in range(TZ)])
    log_e = jnp.log(sum_e) + peak_e
    log_t = jnp.log(sum_t) + peak_t
    loss = 2.0 * log_e - picked + cross / sum_t - log_t

    at = lax.broadcasted_iota(jnp.int32, (NPAIR, NPAIR * SUB), 1) // SUB
    pair = lax.broadcasted_iota(jnp.int32, (NPAIR, NPAIR * SUB), 0)
    spread = jnp.where(at == pair, jnp.broadcast_to(loss, (NPAIR, NPAIR * SUB)), 0.0)
    spread = spread[:, :LANE] + spread[:, LANE:]
    for shift in (64, 32, 16):
        spread = spread + pltpu.roll(spread, shift, 1)
    place = lax.broadcasted_iota(jnp.int32, (NPAIR, LANE), 1) // SUB
    loss_y[sec] = jnp.where(place == sec, spread, 0.0)
    for k, peer in enumerate(sec_peers):
        send(loss_y.at[sec], loss_y.at[sec], y_send.at[k], y_recv.at[sec], peer)
    for peer in sec_peers:
        arrived(loss_y.at[peer[0]], y_recv.at[peer[0]], y_send.at[0])
    total = loss_y[0]
    for u in range(1, NS):
        total = total + loss_y[u]
    tot_v[pl.ds(0, NPAIR)] = total
    tot_v[pl.ds(NPAIR, 8)] = jnp.zeros((8, LANE), F32)
    start = jnp.int32(0)
    for u in range(NS):
        start = start + jnp.where(u < sec, counts[u], 0)
    for k in range(MAXB):
        row = tot_v[pl.ds(start + k, 1), :]
        out_ref[0, pl.ds(k, 1), :] = jnp.where(k < ec_s[0], row, 0.0)
    for copy in sends:
        copy.wait_send()


def body(stream_in, layer_delta, norm_gain, out_embed, exit_blocks, exit_counts, targets):
    feat = stream_in.shape[1]
    any_spec = pl.BlockSpec(memory_space=pl.ANY)
    dma = pltpu.SemaphoreType.DMA
    bf16, i32 = jnp.bfloat16, jnp.int32
    vm = pltpu.VMEM
    return pl.pallas_call(
        kernel,
        out_shape=jax.ShapeDtypeStruct((1, MAXB, BLK), F32),
        in_specs=[any_spec] * 7,
        out_specs=pl.BlockSpec(memory_space=pltpu.VMEM),
        scratch_shapes=[
            pltpu.SMEM((1, MAXB), i32),
            pltpu.SMEM((1,), i32),
            pltpu.SMEM((NS, 1, LANE), i32),
            pltpu.SMEM((NPAIR,), i32),
            pltpu.SMEM((NPAIR,), i32),
            pltpu.SMEM((NPAIR,), i32),
            vm((NC, LANE), F32),
            vm((NB, BLK), i32),
            vm((NB, SUB, feat), bf16),
            vm((1, LANE), i32),
            vm((NS, 1, LANE), i32),
            vm((NC, NS, NB, SUB, LANE), bf16),
            vm((NS, NB, SUB, LANE), F32),
            vm((24, SUB, LANE), F32),
            vm((NT, NC, ROWS, LANE), bf16),
            vm((NT, NC * LANE, VPART), bf16),
            vm((NG, SUB, VPART), F32),
            vm((TX, 8, LANE), F32),
            vm((TZ, 8, LANE), F32),
            vm((24, SUB, LANE), F32),
            vm((NB, SUB, VPART), F32),
            vm((NB, SUB, LANE), F32),
            vm((NB, SUB, LANE), F32),
            vm((NPAIR, SUB, LANE), F32),
            vm((TX, 8, NPAIR * SUB), F32),
            vm((TZ, 8, NPAIR * SUB), F32),
            vm((NS, NPAIR, LANE), F32),
            vm((24, LANE), F32),
            dma((10,)),
            dma((NT,)),
            dma((NS - 1,)),
            dma((NS,)),
            dma((NC, NS - 1)),
            dma((NC, NS)),
            dma((NC * (NT - 1),)),
            dma((NT, NC)),
            dma((4, 3)),
            dma((4, 4)),
            dma((NS - 1,)),
            dma((NS,)),
        ],
        compiler_params=pltpu.CompilerParams(
            collective_id=0, has_side_effects=True, vmem_limit_bytes=48 * 1024 * 1024
        ),
    )(
        exit_blocks,
        exit_counts,
        norm_gain.reshape(NC, LANE),
        targets.reshape(NB, BLK),
        stream_in.reshape(NB, NS, SUB, feat),
        layer_delta.reshape(NB, NS, SUB, feat),
        out_embed.reshape(NT, NC * LANE, VPART),
    )


def solution(mesh):
    placed = (
        P(None, "tp"),
        P("section", None, "tp"),
        P("tp"),
        P(None, "tp"),
        P("section", None),
        P("section"),
        P(),
    )
    return jax.shard_map(
        body, mesh=mesh, in_specs=placed, out_specs=P("section", None, None), check_vma=False
    )
```

```python
import functools
import itertools

import jax
import jax.numpy as jnp
from jax import lax
from jax.experimental import pallas as pl
from jax.experimental.pallas import tpu as pltpu
from jax.sharding import PartitionSpec as P

BLK = 128
MAXB = 4
EPS = 1e-05
NS = 8
TX = 4
TZ = 4
NT = TX * TZ
SUB = BLK // NS
NPAIR = 2 * NS
NB = 4
NG = NPAIR - 1 + NB
ROWS = NG * SUB
LANE = 128
NC = 4
WIDTH = LANE * NC * NT
VPART = 1024
NTILE = 1024
DOWN = 2.0 ** -58
UP = 2.0 ** 58
F32 = jnp.float32
MESH = pl.DeviceIdType.MESH
ORDER = (0, 2, 1, 3)


def long_sign(c):
    return 1 if c % 2 == 0 else -1


def rel_of(c, a, b):
    dx, dz = (a, b) if c < NC // 2 else (b, a)
    return (dx % TX) * TZ + dz % TZ


def step_of(c, axis, sign):
    along_x = (axis == 0) == (c < NC // 2)
    return (sign, 0) if along_x else (0, sign)


def forwards(c, a, b):
    go = long_sign(c)
    if (a, b) == (0, 0):
        return [(0, go), (0, -go), (1, go), (1, -go)]
    if b == 0:
        out = [(0, go)] if a == -go else []
        return out + [(1, go), (1, -go)]
    return [(1, go)] if b == -go else []


def wrap(v):
    v = v % 4
    return v - 4 if v == 3 else v


def events():
    out = []
    for dist in range(1, 5):
        for c in ORDER:
            go = long_sign(c)
            places = [(2, 0), (-go, 0), (go, 0), (2, -go), (2, go), (-go, -go), (go, -go), (0, -go)]
            places += [(-go, go), (go, go), (0, go), (0, 2), (-go, 2), (go, 2), (2, 2)]
            out += [(c, a, b) for a, b in places if abs(a) + abs(b) == dist]
    return out


def plan():
    ready = {(0, 0): 2, (0, 1): 2}
    queue = [(0, 0), (0, 1)]
    steps = []
    for c, a, b in events():
        steps.append(("wait", c, a, b))
        key = (rel_of(c, a, b), c // 2)
        ready[key] = ready.get(key, 0) + 1
        if ready[key] == 2:
            queue.append(key)
        if queue:
            steps.append(("dot",) + queue.pop(0))
    return steps + [("dot",) + key for key in queue]


STEPS = plan()
FIRST_USE = list(dict.fromkeys(s[1] for s in STEPS if s[0] == "dot"))


def merge(parts):
    peak_e = functools.reduce(jnp.maximum, [p[0:1] for p in parts])
    peak_t = functools.reduce(jnp.maximum, [p[2:3] for p in parts])
    sum_e = sum_t = cross = picked = 0.0
    for p in parts:
        fe = jnp.exp(p[0:1] - peak_e)
        ft = jnp.exp(p[2:3] - peak_t)
        sum_e = sum_e + p[1:2] * fe
        sum_t = sum_t + p[3:4] * ft
        cross = cross + p[4:5] * ft
        picked = picked + p[5:6]
    return peak_e, sum_e, peak_t, sum_t, cross, picked


def kernel(
    eb_hbm, ec_hbm, gain_hbm, tgt_hbm, stream_hbm, delta_hbm, w_hbm, out_ref,
    eb_s, ec_s, meta_s, own_s, blk_s, grp_s,
    gain_v, tgt_v, stream_v, delta_v, abuf, hid, sq, gath, wv, acc,
    ss_x, ss_z, scale_v, prob_v, tstat, tcol, pst, st_x, st_z, loss_y, tot_v,
    loc_sem, w_sem, meta_send, meta_recv, a_send, a_recv, g_send, g_recv, ex_send, ex_recv, y_send, y_recv,
):
    sec = lax.axis_index("section")
    tp = lax.axis_index("tp")
    px, pz = tp // TZ, tp % TZ

    def plane(dx, dz):
        return (sec, ((px + dx) % TX) * TZ + (pz + dz) % TZ)

    sec_peers = [((sec + k) % NS, tp) for k in range(1, NS)]
    x_peers = [plane(k, 0) for k in range(1, TX)]
    z_peers = [plane(0, k) for k in range(1, TZ)]
    everyone = sec_peers + x_peers + z_peers

    barrier = pltpu.get_barrier_semaphore()
    for peer in everyone:
        pl.semaphore_signal(barrier, inc=1, device_id=peer, device_id_type=MESH)

    local = [
        pltpu.make_async_copy(eb_hbm, eb_s, loc_sem.at[0]),
        pltpu.make_async_copy(ec_hbm, ec_s, loc_sem.at[1]),
        pltpu.make_async_copy(stream_hbm.at[:, sec], stream_v, loc_sem.at[2]),
        pltpu.make_async_copy(gain_hbm, gain_v, loc_sem.at[3]),
        pltpu.make_async_copy(tgt_hbm, tgt_v, loc_sem.at[4]),
    ]
    own_delta = [
        pltpu.make_async_copy(
            delta_hbm.at[:, sec, :, pl.ds(c * LANE, LANE)], abuf.at[c, sec], loc_sem.at[5 + c]
        )
        for c in range(NC)
    ]
    all_delta = pltpu.make_async_copy(delta_hbm, delta_v, loc_sem.at[10])
    for copy in local[:2] + [all_delta] + local[2:] + own_delta:
        copy.start()

    local[0].wait()
    local[1].wait()
    for k in range(MAXB):
        meta_s[sec, 0, k] = eb_s[0, k]
    meta_s[sec, 0, MAXB] = ec_s[0, 0]

    all_delta.wait()
    pl.semaphore_wait(barrier, len(everyone))

    sends = []

    def send(src, dst, send_sem, recv_sem, peer):
        copy = pltpu.make_async_remote_copy(
            src_ref=src, dst_ref=dst, send_sem=send_sem, recv_sem=recv_sem,
            device_id=peer, device_id_type=MESH,
        )
        copy.start()
        sends.append(copy)

    def arrived(dst, recv_sem, any_sem):
        pltpu.make_async_remote_copy(
            src_ref=dst, dst_ref=dst, send_sem=any_sem, recv_sem=recv_sem,
            device_id=x_peers[0], device_id_type=MESH,
        ).wait_recv()

    for k, peer in enumerate(sec_peers):
        send(meta_s.at[sec], meta_s.at[sec], meta_send.at[k], meta_recv.at[sec], peer)
    for c in ORDER:
        for k, peer in enumerate(sec_peers):
            send(
                delta_v.at[:, peer[0], :, pl.ds(c * LANE, LANE)], abuf.at[c, sec],
                a_send.at[c, k], a_recv.at[c, sec], peer,
            )

    w_copies = {}
    for i, rel in enumerate(FIRST_USE):
        src_tp = ((px + rel // TZ) % TX) * TZ + (pz + rel % TZ) % TZ
        w_copies[rel] = pltpu.make_async_copy(w_hbm.at[src_tp], wv.at[rel], w_sem.at[i])
        w_copies[rel].start()

    for peer in sec_peers:
        arrived(meta_s.at[peer[0]], meta_recv.at[peer[0]], meta_send.at[0])
    counts = [meta_s[u, 0, MAXB] for u in range(NS)]
    offs = [jnp.int32(0)]
    for u in range(NS - 1):
        offs.append(offs[-1] + counts[u])
    for j in range(NPAIR):
        owner = jnp.int32(0)
        base = jnp.int32(0)
        for u in range(1, NS):
            owner = jnp.where(offs[u] <= j, u, owner)
            base = jnp.where(offs[u] <= j, offs[u], base)
        block = meta_s[owner, 0, jnp.minimum(j - base, MAXB - 1)]
        own_s[j] = owner
        blk_s[j] = block
        grp_s[j] = j if j < NPAIR - 1 else NPAIR - 1 + block

    local[2].wait()
    local[3].wait()
    local[4].wait()
    lane_r = lax.broadcasted_iota(jnp.int32, (SUB, LANE), 1)
    sub_r = lax.broadcasted_iota(jnp.int32, (SUB, LANE), 0)
    mine = lane_r == sec * SUB + sub_r
    for b in range(NB):
        row = jnp.broadcast_to(tgt_v[b : b + 1, :].astype(F32), (SUB, LANE))
        col = jnp.sum(jnp.where(mine, row, 0.0), axis=1, keepdims=True)
        tcol[b] = jnp.broadcast_to(col, (SUB, LANE)) - (tp * VPART).astype(F32)

    hop = itertools.count()

    def pass_on(c, a, b):
        rel = rel_of(c, a, b)
        for axis, sign in forwards(c, a, b):
            aa, bb = (wrap(a - sign), b) if axis == 0 else (a, wrap(b - sign))
            there = rel_of(c, aa, bb)
            send(
                gath.at[rel, c], gath.at[there, c],
                g_send.at[next(hop)], g_recv.at[there, c],
                plane(*step_of(c, axis, sign)),
            )

    for n, c in enumerate(ORDER):
        own_delta[c].wait()
        for peer in sec_peers:
            arrived(abuf.at[c, peer[0]], a_recv.at[c, peer[0]], a_send.at[0, 0])
        lanes = pl.ds(c * LANE, LANE)
        state = stream_v[:, :, lanes].astype(F32)
        for u in range(NS):
            state = state + abuf[c, u].astype(F32)
            hid[u] = state
        gain = gain_v[c : c + 1, :] * DOWN

        def put(g, rows, c=c, n=n, gain=gain):
            sq[g] = rows * rows if n == 0 else sq[g] + rows * rows
            gath[0, c, pl.ds(g * SUB, SUB), :] = (rows * gain).astype(jnp.bfloat16)

        for j in range(NPAIR - 1):
            put(j, hid[own_s[j], blk_s[j]])
        for b in range(NB):
            put(NPAIR - 1 + b, hid[NS - 1, b])
        pass_on(c, 0, 0)

    for g in range(NG, 24):
        sq[g] = jnp.zeros((SUB, LANE), F32)
    sums = []
    for q in range(3):
        part = sq[pl.ds(q * 8, 8)].reshape(LANE, LANE)
        sums.append(jnp.sum(part.T, axis=0, keepdims=True))
    ss_x[px] = jnp.concatenate(sums + [jnp.zeros((5, LANE), F32)], axis=0)

    def share(buf, place, peers, stage):
        for k, peer in enumerate(peers):
            send(buf.at[place], buf.at[place], ex_send.at[stage, k], ex_recv.at[stage, place], peer)

    def collect(buf, place, stage):
        for k in range(1, 4):
            there = (place + k) % 4
            arrived(buf.at[there], ex_recv.at[stage, there], ex_send.at[stage, 0])

    share(ss_x, px, x_peers, 0)

    seen = set()
    waits = 0
    for step in STEPS:
        if step[0] == "wait":
            _, c, a, b = step
            rel = rel_of(c, a, b)
            arrived(gath.at[rel, c], g_recv.at[rel, c], g_send.at[0])
            pass_on(c, a, b)
            waits += 1
            if waits == 12:
                collect(ss_x, px, 0)
                ss_z[pz] = ss_x[0] + ss_x[1] + ss_x[2] + ss_x[3]
                share(ss_z, pz, z_peers, 1)
            if waits == 36:
                collect(ss_z, pz, 1)
                total = ss_z[0] + ss_z[1] + ss_z[2] + ss_z[3]
                scale = lax.rsqrt(total / WIDTH + EPS) * UP
                for q in range(3):
                    wide = jnp.broadcast_to(scale[q : q + 1, :], (LANE, LANE)).T
                    scale_v[pl.ds(q * 8, 8)] = wide.reshape(8, SUB, LANE)
        else:
            _, rel, half = step
            if rel not in seen:
                w_copies[rel].wait()
            first = not seen
            seen.add(rel)

            def tile(n, carry, rel=rel, half=half, first=first):
                cols = pl.ds(pl.multiple_of(n * NTILE, NTILE), NTILE)
                lhs = jnp.concatenate([gath[rel, 2 * half], gath[rel, 2 * half + 1]], axis=1)
                rhs = wv[rel, pl.ds(half * 2 * LANE, 2 * LANE), cols]
                part = jnp.dot(lhs, rhs, preferred_element_type=F32).reshape(NG, SUB, NTILE)
                acc[:, :, cols] = part if first else acc[:, :, cols] + part
                return carry

            lax.fori_loop(0, VPART // NTILE, tile, 0)

    def wide8(v):
        return jnp.concatenate([v] * (VPART // LANE), axis=1)

    def teach(b, carry):
        logit = acc[NPAIR - 1 + b] * wide8(scale_v[NPAIR - 1 + b])
        peak = jnp.max(logit, axis=1, keepdims=True)
        weight = jnp.exp(logit - peak)
        prob_v[b] = weight
        total = jnp.sum(weight, axis=1, keepdims=True)
        tstat[b] = jnp.where(lane_r == 2, peak, jnp.where(lane_r == 3, total, 0.0))
        return carry

    lax.fori_loop(0, NB, teach, 0, unroll=True)
    column = lax.broadcasted_iota(jnp.int32, (SUB, VPART), 1).astype(F32)

    def leave(j, carry):
        block = blk_s[j]
        group = grp_s[j]
        exit_logit = acc[group] * wide8(scale_v[group])
        teach_logit = acc[NPAIR - 1 + block] * wide8(scale_v[NPAIR - 1 + block])
        weight = prob_v[block]
        peak = jnp.max(exit_logit, axis=1, keepdims=True)
        total = jnp.sum(jnp.exp(exit_logit - peak), axis=1, keepdims=True)
        cross = jnp.sum(weight * (teach_logit - exit_logit), axis=1, keepdims=True)
        hit = wide8(tcol[block]) == column
        picked = jnp.sum(jnp.where(hit, exit_logit, 0.0), axis=1, keepdims=True)
        out = tstat[block]
        for k, v in ((0, peak), (1, total), (4, cross), (5, picked)):
            out = jnp.where(lane_r == k, v, out)
        pst[j] = out
        return carry

    lax.fori_loop(0, NPAIR, leave, 0, unroll=4)
    stats = [pst[pl.ds(q * 8, 8)].reshape(LANE, LANE).T[0:8, :] for q in range(2)]
    st_x[px] = jnp.concatenate(stats, axis=1)
    share(st_x, px, x_peers, 2)
    collect(st_x, px, 2)
    joined = merge([st_x[i] for i in range(TX)])
    st_z[pz] = jnp.concatenate(list(joined) + [jnp.zeros((2, NPAIR * SUB), F32)], axis=0)
    share(st_z, pz, z_peers, 3)
    collect(st_z, pz, 3)
    peak_e, sum_e, peak_t, sum_t, cross, picked = merge([st_z[i] for i in range(TZ)])
    log_e = jnp.log(sum_e) + peak_e
    log_t = jnp.log(sum_t) + peak_t
    loss = 2.0 * log_e - picked + cross / sum_t - log_t

    at = lax.broadcasted_iota(jnp.int32, (NPAIR, NPAIR * SUB), 1) // SUB
    pair = lax.broadcasted_iota(jnp.int32, (NPAIR, NPAIR * SUB), 0)
    spread = jnp.where(at == pair, jnp.broadcast_to(loss, (NPAIR, NPAIR * SUB)), 0.0)
    spread = spread[:, :LANE] + spread[:, LANE:]
    for shift in (64, 32, 16):
        spread = spread + pltpu.roll(spread, shift, 1)
    place = lax.broadcasted_iota(jnp.int32, (NPAIR, LANE), 1) // SUB
    loss_y[sec] = jnp.where(place == sec, spread, 0.0)
    for k, peer in enumerate(sec_peers):
        send(loss_y.at[sec], loss_y.at[sec], y_send.at[k], y_recv.at[sec], peer)
    for peer in sec_peers:
        arrived(loss_y.at[peer[0]], y_recv.at[peer[0]], y_send.at[0])
    total = loss_y[0]
    for u in range(1, NS):
        total = total + loss_y[u]
    tot_v[pl.ds(0, NPAIR)] = total
    tot_v[pl.ds(NPAIR, 8)] = jnp.zeros((8, LANE), F32)
    start = jnp.int32(0)
    for u in range(NS):
        start = start + jnp.where(u < sec, counts[u], 0)
    for k in range(MAXB):
        row = tot_v[pl.ds(start + k, 1), :]
        out_ref[0, pl.ds(k, 1), :] = jnp.where(k < ec_s[0, 0], row, 0.0)
    for copy in sends:
        copy.wait_send()


def body(stream_in, layer_delta, norm_gain, out_embed, exit_blocks, exit_counts, targets):
    feat = stream_in.shape[1]
    any_spec = pl.BlockSpec(memory_space=pl.ANY)
    dma = pltpu.SemaphoreType.DMA
    bf16, i32 = jnp.bfloat16, jnp.int32
    vm = pltpu.VMEM
    return pl.pallas_call(
        kernel,
        out_shape=jax.ShapeDtypeStruct((1, MAXB, BLK), F32),
        in_specs=[any_spec] * 7,
        out_specs=pl.BlockSpec(memory_space=pltpu.VMEM),
        scratch_shapes=[
            pltpu.SMEM((1, MAXB), i32),
            pltpu.SMEM((1, 1), i32),
            pltpu.SMEM((NS, 1, LANE), i32),
            pltpu.SMEM((NPAIR,), i32),
            pltpu.SMEM((NPAIR,), i32),
            pltpu.SMEM((NPAIR,), i32),
            vm((NC, LANE), F32),
            vm((NB, BLK), i32),
            vm((NB, SUB, feat), bf16),
            vm((NB, NS, SUB, feat), bf16),
            vm((NC, NS, NB, SUB, LANE), bf16),
            vm((NS, NB, SUB, LANE), F32),
            vm((24, SUB, LANE), F32),
            vm((NT, NC, ROWS, LANE), bf16),
            vm((NT, NC * LANE, VPART), bf16),
            vm((NG, SUB, VPART), F32),
            vm((TX, 8, LANE), F32),
            vm((TZ, 8, LANE), F32),
            vm((24, SUB, LANE), F32),
            vm((NB, SUB, VPART), F32),
            vm((NB, SUB, LANE), F32),
            vm((NB, SUB, LANE), F32),
            vm((NPAIR, SUB, LANE), F32),
            vm((TX, 8, NPAIR * SUB), F32),
            vm((TZ, 8, NPAIR * SUB), F32),
            vm((NS, NPAIR, LANE), F32),
            vm((24, LANE), F32),
            dma((11,)),
            dma((NT,)),
            dma((NS - 1,)),
            dma((NS,)),
            dma((NC, NS - 1)),
            dma((NC, NS)),
            dma((NC * (NT - 1),)),
            dma((NT, NC)),
            dma((4, 3)),
            dma((4, 4)),
            dma((NS - 1,)),
            dma((NS,)),
        ],
        compiler_params=pltpu.CompilerParams(
            collective_id=0, has_side_effects=True, vmem_limit_bytes=60 * 1024 * 1024
        ),
    )(
        exit_blocks,
        exit_counts.reshape(1, 1),
        norm_gain.reshape(NC, LANE),
        targets.reshape(NB, BLK),
        stream_in.reshape(NB, NS, SUB, feat),
        layer_delta.reshape(NB, NS, SUB, feat),
        out_embed.reshape(NT, NC * LANE, VPART),
    )


def solution(mesh):
    placed = (
        P(None, "tp"),
        P("section", None, "tp"),
        P("tp"),
        P(None, "tp"),
        P("section", None),
        P("section"),
        P(),
    )
    return jax.shard_map(
        body, mesh=mesh, in_specs=placed, out_specs=P("section", None, None), check_vma=False
    )
```

```python
import functools
import heapq
import itertools

import jax
import jax.numpy as jnp
from jax import lax
from jax.experimental import pallas as pl
from jax.experimental.pallas import tpu as pltpu
from jax.sharding import PartitionSpec as P

BLK = 128
MAXB = 4
EPS = 1e-05
NS = 8
TX = 4
TZ = 4
NT = TX * TZ
SUB = BLK // NS
NPAIR = 2 * NS
NB = 4
NG = NPAIR - 1 + NB
ROWS = NG * SUB
LANE = 128
NC = 4
WIDTH = LANE * NC * NT
VPART = 1024
NTILE = 1024
DOWN = 2.0 ** -58
UP = 2.0 ** 58
F32 = jnp.float32
MESH = pl.DeviceIdType.MESH
ORDER = (0, 2, 3, 1)
HOP, LAND, GAP, DOT, DEPTH = 1.68, 2.2, 1.3, 0.33, 1


def long_sign(c):
    return 1 if c % 2 == 0 else -1


def rel_of(c, a, b):
    dx, dz = (a, b) if c < NC // 2 else (b, a)
    return (dx % TX) * TZ + dz % TZ


def step_of(c, axis, sign):
    along_x = (axis == 0) == (c < NC // 2)
    return (sign, 0) if along_x else (0, sign)


def forwards(c, a, b):
    go = long_sign(c)
    if (a, b) == (0, 0):
        return [(0, go), (0, -go), (1, go), (1, -go)]
    if b == 0:
        out = [(0, go)] if a == -go else []
        return out + [(1, go), (1, -go)]
    return [(1, go)] if b == -go else []


def wrap(v):
    v = v % 4
    return v - 4 if v == 3 else v


def ahead(c, a, b):
    return max([1 + ahead(c, *moved(a, b, axis, sign)) for axis, sign in forwards(c, a, b)], default=0)


def moved(a, b, axis, sign):
    return (wrap(a - sign), b) if axis == 0 else (a, wrap(b - sign))


def plan():
    tick = itertools.count()
    heap = [(GAP * i, 0, next(tick), ("own", c, 0, 0)) for i, c in enumerate(ORDER)]
    pending, loaded, free, ready = {}, {}, {}, {}
    steps, dots = [], []

    def feed(hop, now):
        queue = pending.get(hop, [])
        while queue and loaded.get(hop, 0) <= DEPTH:
            queue.sort()
            _, _, _, c, a, b, axis, sign = queue.pop(0)
            free[hop] = max(now, free.get(hop, 0.0)) + HOP
            loaded[hop] = loaded.get(hop, 0) + 1
            steps.append(("send", c, a, b, axis, sign))
            heapq.heappush(heap, (free[hop], 2, next(tick), ("free", hop)))
            landed = ("wait", c) + moved(a, b, axis, sign)
            heapq.heappush(heap, (free[hop] + LAND, 1, next(tick), landed))

    now = 0.0
    while heap:
        at, _, _, event = heapq.heappop(heap)
        now = max(now, at)
        if event[0] == "free":
            loaded[event[1]] -= 1
            feed(event[1], at)
            continue
        steps.append(event)
        _, c, a, b = event
        for axis, sign in forwards(c, a, b):
            hop = step_of(c, axis, sign)
            rank = (-ahead(c, *moved(a, b, axis, sign)), ORDER.index(c), next(tick))
            pending.setdefault(hop, []).append(rank + (c, a, b, axis, sign))
        for axis, sign in forwards(c, a, b):
            feed(step_of(c, axis, sign), now)
        key = (rel_of(c, a, b), c // 2)
        ready[key] = ready.get(key, 0) + 1
        if ready[key] == 2:
            dots.append(("dot",) + key)
        if dots and event[0] == "wait":
            steps.append(dots.pop(0))
            now += DOT
    return steps + dots


STEPS = plan()
FIRST_USE = list(dict.fromkeys(s[1] for s in STEPS if s[0] == "dot"))


FAR_FIRST = sorted(range(1, NT), key=lambda k: -abs(wrap(k // TZ)) - abs(wrap(k % TZ)))


def kernel(
    eb_hbm, ec_hbm, gain_hbm, tgt_hbm, stream_hbm, delta_hbm, w_hbm, out_ref,
    eb_s, ec_s, meta_s, own_s, blk_s, grp_s,
    gain_v, tgt_v, stream_v, delta_v, abuf, hid, sq, gath, wv, acc,
    ss_x, ss_z, scale_v, prob_v, tstat, tcol, pst, stat_v, loss_y, tot_v,
    loc_sem, w_sem, meta_send, meta_recv, a_send, a_recv, g_send, g_recv, ex_send, ex_recv, st_send, st_recv, y_send, y_recv,
):
    sec = lax.axis_index("section")
    tp = lax.axis_index("tp")
    px, pz = tp // TZ, tp % TZ

    def plane(dx, dz):
        return (sec, ((px + dx) % TX) * TZ + (pz + dz) % TZ)

    sec_peers = [((sec + k) % NS, tp) for k in (4, 3, 5, 2, 6, 1, 7)]
    x_peers = [plane(k, 0) for k in range(1, TX)]
    z_peers = [plane(0, k) for k in range(1, TZ)]
    tp_peers = [plane(k // TZ, k % TZ) for k in FAR_FIRST]
    everyone = sec_peers + x_peers + z_peers

    barrier = pltpu.get_barrier_semaphore()
    for peer in everyone:
        pl.semaphore_signal(barrier, inc=1, device_id=peer, device_id_type=MESH)

    local = [
        pltpu.make_async_copy(eb_hbm, eb_s, loc_sem.at[0]),
        pltpu.make_async_copy(ec_hbm, ec_s, loc_sem.at[1]),
        pltpu.make_async_copy(stream_hbm.at[:, sec], stream_v, loc_sem.at[2]),
        pltpu.make_async_copy(gain_hbm, gain_v, loc_sem.at[3]),
        pltpu.make_async_copy(tgt_hbm, tgt_v, loc_sem.at[4]),
    ]
    own_delta = [
        pltpu.make_async_copy(
            delta_hbm.at[:, sec, :, pl.ds(c * LANE, LANE)], abuf.at[c, sec], loc_sem.at[5 + c]
        )
        for c in range(NC)
    ]
    all_delta = pltpu.make_async_copy(delta_hbm, delta_v, loc_sem.at[10])
    for copy in local[:2] + [all_delta] + local[2:] + own_delta:
        copy.start()

    local[0].wait()
    local[1].wait()
    for k in range(MAXB):
        meta_s[sec, 0, k] = eb_s[0, k]
    meta_s[sec, 0, MAXB] = ec_s[0, 0]

    all_delta.wait()
    pl.semaphore_wait(barrier, len(everyone))

    sends = []

    def send(src, dst, send_sem, recv_sem, peer):
        copy = pltpu.make_async_remote_copy(
            src_ref=src, dst_ref=dst, send_sem=send_sem, recv_sem=recv_sem,
            device_id=peer, device_id_type=MESH,
        )
        copy.start()
        sends.append(copy)

    def arrived(dst, recv_sem, any_sem):
        pltpu.make_async_remote_copy(
            src_ref=dst, dst_ref=dst, send_sem=any_sem, recv_sem=recv_sem,
            device_id=x_peers[0], device_id_type=MESH,
        ).wait_recv()

    for k, peer in enumerate(sec_peers):
        send(meta_s.at[sec], meta_s.at[sec], meta_send.at[k], meta_recv.at[sec], peer)
    for c in ORDER:
        for k, peer in enumerate(sec_peers):
            send(
                delta_v.at[:, peer[0], :, pl.ds(c * LANE, LANE)], abuf.at[c, sec],
                a_send.at[c, k], a_recv.at[c, sec], peer,
            )

    w_copies = {}
    for i, rel in enumerate(FIRST_USE):
        src_tp = ((px + rel // TZ) % TX) * TZ + (pz + rel % TZ) % TZ
        w_copies[rel] = pltpu.make_async_copy(w_hbm.at[src_tp], wv.at[rel], w_sem.at[i])
        w_copies[rel].start()

    for peer in sec_peers:
        arrived(meta_s.at[peer[0]], meta_recv.at[peer[0]], meta_send.at[0])
    counts = [meta_s[u, 0, MAXB] for u in range(NS)]
    offs = [jnp.int32(0)]
    for u in range(NS - 1):
        offs.append(offs[-1] + counts[u])
    for j in range(NPAIR):
        owner = jnp.int32(0)
        base = jnp.int32(0)
        for u in range(1, NS):
            owner = jnp.where(offs[u] <= j, u, owner)
            base = jnp.where(offs[u] <= j, offs[u], base)
        block = meta_s[owner, 0, jnp.minimum(j - base, MAXB - 1)]
        own_s[j] = owner
        blk_s[j] = block
        grp_s[j] = j if j < NPAIR - 1 else NPAIR - 1 + block

    local[2].wait()
    local[3].wait()
    local[4].wait()
    lane_r = lax.broadcasted_iota(jnp.int32, (SUB, LANE), 1)
    sub_r = lax.broadcasted_iota(jnp.int32, (SUB, LANE), 0)
    mine = lane_r == sec * SUB + sub_r
    for b in range(NB):
        row = jnp.broadcast_to(tgt_v[b : b + 1, :].astype(F32), (SUB, LANE))
        col = jnp.sum(jnp.where(mine, row, 0.0), axis=1, keepdims=True)
        tcol[b] = jnp.broadcast_to(col, (SUB, LANE)) - (tp * VPART).astype(F32)

    hop = itertools.count()

    def pass_on(c, a, b, axis, sign):
        there = rel_of(c, *moved(a, b, axis, sign))
        send(
            gath.at[rel_of(c, a, b), c], gath.at[there, c],
            g_send.at[next(hop)], g_recv.at[there, c],
            plane(*step_of(c, axis, sign)),
        )

    def own_shard(c):
        own_delta[c].wait()
        for peer in sec_peers:
            arrived(abuf.at[c, peer[0]], a_recv.at[c, peer[0]], a_send.at[0, 0])
        state = stream_v[:, :, pl.ds(c * LANE, LANE)].astype(F32)
        for u in range(NS):
            state = state + abuf[c, u].astype(F32)
            hid[u] = state
        gain = gain_v[c : c + 1, :] * DOWN

        def put(g, rows):
            sq[g] = rows * rows if c == ORDER[0] else sq[g] + rows * rows
            gath[0, c, pl.ds(g * SUB, SUB), :] = (rows * gain).astype(jnp.bfloat16)

        for j in range(NPAIR - 1):
            put(j, hid[own_s[j], blk_s[j]])
        for b in range(NB):
            put(NPAIR - 1 + b, hid[NS - 1, b])

    def share(buf, place, peers, stage):
        for k, peer in enumerate(peers):
            send(buf.at[place], buf.at[place], ex_send.at[stage, k], ex_recv.at[stage, place], peer)

    def collect(buf, place, stage):
        for k in range(1, 4):
            there = (place + k) % 4
            arrived(buf.at[there], ex_recv.at[stage, there], ex_send.at[stage, 0])

    def squares():
        for g in range(NG, 24):
            sq[g] = jnp.zeros((SUB, LANE), F32)
        sums = []
        for q in range(3):
            part = sq[pl.ds(q * 8, 8)].reshape(LANE, LANE)
            sums.append(jnp.sum(part.T, axis=0, keepdims=True))
        ss_x[px] = jnp.concatenate(sums + [jnp.zeros((5, LANE), F32)], axis=0)
        share(ss_x, px, x_peers, 0)

    seen = set()
    waits = owns = 0
    for step in STEPS:
        if step[0] == "own":
            own_shard(step[1])
            owns += 1
            first_wait = waits
        elif step[0] == "send":
            pass_on(*step[1:])
        elif step[0] == "wait":
            _, c, a, b = step
            rel = rel_of(c, a, b)
            arrived(gath.at[rel, c], g_recv.at[rel, c], g_send.at[0])
            waits += 1
            if owns == NC and waits == first_wait + 1:
                squares()
            if owns == NC and waits == first_wait + 10:
                collect(ss_x, px, 0)
                ss_z[pz] = ss_x[0] + ss_x[1] + ss_x[2] + ss_x[3]
                share(ss_z, pz, z_peers, 1)
            if owns == NC and waits == first_wait + 24:
                collect(ss_z, pz, 1)
                total = ss_z[0] + ss_z[1] + ss_z[2] + ss_z[3]
                scale = lax.rsqrt(total / WIDTH + EPS) * UP
                for q in range(3):
                    wide = jnp.broadcast_to(scale[q : q + 1, :], (LANE, LANE)).T
                    scale_v[pl.ds(q * 8, 8)] = wide.reshape(8, SUB, LANE)
        else:
            _, rel, half = step
            if rel not in seen:
                w_copies[rel].wait()
            first = not seen
            seen.add(rel)

            def tile(n, carry, rel=rel, half=half, first=first):
                cols = pl.ds(pl.multiple_of(n * NTILE, NTILE), NTILE)
                lhs = jnp.concatenate([gath[rel, 2 * half], gath[rel, 2 * half + 1]], axis=1)
                rhs = wv[rel, pl.ds(half * 2 * LANE, 2 * LANE), cols]
                part = jnp.dot(lhs, rhs, preferred_element_type=F32).reshape(NG, SUB, NTILE)
                acc[:, :, cols] = part if first else acc[:, :, cols] + part
                return carry

            lax.fori_loop(0, VPART // NTILE, tile, 0)

    def wide8(v):
        return jnp.concatenate([v] * (VPART // LANE), axis=1)

    def teach(b, carry):
        logit = acc[NPAIR - 1 + b] * wide8(scale_v[NPAIR - 1 + b])
        peak = jnp.max(logit, axis=1, keepdims=True)
        weight = jnp.exp(logit - peak)
        prob_v[b] = weight
        total = jnp.sum(weight, axis=1, keepdims=True)
        tstat[b] = jnp.where(lane_r == 2, peak, jnp.where(lane_r == 3, total, 0.0))
        return carry

    lax.fori_loop(0, NB, teach, 0, unroll=True)
    column = lax.broadcasted_iota(jnp.int32, (SUB, VPART), 1).astype(F32)

    def leave(j, carry):
        block = blk_s[j]
        group = grp_s[j]
        exit_logit = acc[group] * wide8(scale_v[group])
        teach_logit = acc[NPAIR - 1 + block] * wide8(scale_v[NPAIR - 1 + block])
        weight = prob_v[block]
        peak = jnp.max(exit_logit, axis=1, keepdims=True)
        total = jnp.sum(jnp.exp(exit_logit - peak), axis=1, keepdims=True)
        cross = jnp.sum(weight * (teach_logit - exit_logit), axis=1, keepdims=True)
        hit = wide8(tcol[block]) == column
        picked = jnp.sum(jnp.where(hit, exit_logit, 0.0), axis=1, keepdims=True)
        out = tstat[block]
        for k, v in ((0, peak), (1, total), (4, cross), (5, picked)):
            out = jnp.where(lane_r == k, v, out)
        pst[j] = out
        return carry

    lax.fori_loop(0, NPAIR, leave, 0, unroll=4)
    halves = []
    for q in range(2):
        st = pst[pl.ds(q * 8, 8)].reshape(LANE, LANE).T
        lse_e = st[0:1, :] + jnp.log(st[1:2, :])
        lse_t = st[2:3, :] + jnp.log(st[3:4, :])
        halves += [lse_e, lse_t, st[4:5, :] / st[3:4, :], st[5:6, :]]
    stat_v[tp] = jnp.concatenate(halves, axis=0)
    for k, (_, there) in enumerate(tp_peers):
        send(stat_v.at[tp], stat_v.at[tp], st_send.at[k], st_recv.at[tp], (sec, there))
    for _, there in tp_peers:
        arrived(stat_v.at[there], st_recv.at[there], st_send.at[0])
    parts = [stat_v[i] for i in range(NT)]
    peak = functools.reduce(jnp.maximum, parts)
    mass = picked = cross = 0.0
    for p in parts:
        share_of = jnp.exp(p - peak)
        mass = mass + share_of
        cross = cross + pltpu.roll(share_of, 1, 0) * p
        picked = picked + p
    lse = peak + jnp.log(mass)
    loss = jnp.concatenate(
        [
            2.0 * lse[q : q + 1] - picked[q + 3 : q + 4] + cross[q + 2 : q + 3] / mass[q + 1 : q + 2] - lse[q + 1 : q + 2]
            for q in (0, 4)
        ],
        axis=1,
    )

    at = lax.broadcasted_iota(jnp.int32, (NPAIR, NPAIR * SUB), 1) // SUB
    pair = lax.broadcasted_iota(jnp.int32, (NPAIR, NPAIR * SUB), 0)
    spread = jnp.where(at == pair, jnp.broadcast_to(loss, (NPAIR, NPAIR * SUB)), 0.0)
    spread = spread[:, :LANE] + spread[:, LANE:]
    for shift in (64, 32, 16):
        spread = spread + pltpu.roll(spread, shift, 1)
    place = lax.broadcasted_iota(jnp.int32, (NPAIR, LANE), 1) // SUB
    low, high = spread[: NPAIR // 2], spread[NPAIR // 2 :]
    place = place[: NPAIR // 2]
    loss_y[sec] = jnp.where(place == 0, low, jnp.where(place == 1, high, 0.0))
    for k, peer in enumerate(sec_peers):
        send(loss_y.at[sec], loss_y.at[sec], y_send.at[k], y_recv.at[sec], peer)
    for peer in sec_peers:
        arrived(loss_y.at[peer[0]], y_recv.at[peer[0]], y_send.at[0])
    low = high = jnp.zeros((NPAIR // 2, LANE), F32)
    for u in range(NS):
        low = jnp.where(place == u, pltpu.roll(loss_y[u], SUB * u, 1), low)
        high = jnp.where(place == u, pltpu.roll(loss_y[u], (SUB * (u - 1)) % LANE, 1), high)
    tot_v[pl.ds(0, NPAIR // 2)] = low
    tot_v[pl.ds(NPAIR // 2, NPAIR // 2)] = high
    tot_v[pl.ds(NPAIR, 8)] = jnp.zeros((8, LANE), F32)
    start = jnp.int32(0)
    for u in range(NS):
        start = start + jnp.where(u < sec, counts[u], 0)
    for k in range(MAXB):
        row = tot_v[pl.ds(start + k, 1), :]
        out_ref[0, pl.ds(k, 1), :] = jnp.where(k < ec_s[0, 0], row, 0.0)
    for copy in sends:
        copy.wait_send()


def body(stream_in, layer_delta, norm_gain, out_embed, exit_blocks, exit_counts, targets):
    feat = stream_in.shape[1]
    any_spec = pl.BlockSpec(memory_space=pl.ANY)
    dma = pltpu.SemaphoreType.DMA
    bf16, i32 = jnp.bfloat16, jnp.int32
    vm = pltpu.VMEM
    return pl.pallas_call(
        kernel,
        out_shape=jax.ShapeDtypeStruct((1, MAXB, BLK), F32),
        in_specs=[any_spec] * 7,
        out_specs=pl.BlockSpec(memory_space=pltpu.VMEM),
        scratch_shapes=[
            pltpu.SMEM((1, MAXB), i32),
            pltpu.SMEM((1, 1), i32),
            pltpu.SMEM((NS, 1, LANE), i32),
            pltpu.SMEM((NPAIR,), i32),
            pltpu.SMEM((NPAIR,), i32),
            pltpu.SMEM((NPAIR,), i32),
            vm((NC, LANE), F32),
            vm((NB, BLK), i32),
            vm((NB, SUB, feat), bf16),
            vm((NB, NS, SUB, feat), bf16),
            vm((NC, NS, NB, SUB, LANE), bf16),
            vm((NS, NB, SUB, LANE), F32),
            vm((24, SUB, LANE), F32),
            vm((NT, NC, ROWS, LANE), bf16),
            vm((NT, NC * LANE, VPART), bf16),
            vm((NG, SUB, VPART), F32),
            vm((TX, 8, LANE), F32),
            vm((TZ, 8, LANE), F32),
            vm((24, SUB, LANE), F32),
            vm((NB, SUB, VPART), F32),
            vm((NB, SUB, LANE), F32),
            vm((NB, SUB, LANE), F32),
            vm((NPAIR, SUB, LANE), F32),
            vm((NT, 8, LANE), F32),
            vm((NS, NPAIR // 2, LANE), F32),
            vm((24, LANE), F32),
            dma((11,)),
            dma((NT,)),
            dma((NS - 1,)),
            dma((NS,)),
            dma((NC, NS - 1)),
            dma((NC, NS)),
            dma((NC * (NT - 1),)),
            dma((NT, NC)),
            dma((2, 3)),
            dma((2, 4)),
            dma((NT - 1,)),
            dma((NT,)),
            dma((NS - 1,)),
            dma((NS,)),
        ],
        compiler_params=pltpu.CompilerParams(
            collective_id=0, has_side_effects=True, vmem_limit_bytes=60 * 1024 * 1024
        ),
    )(
        exit_blocks,
        exit_counts.reshape(1, 1),
        norm_gain.reshape(NC, LANE),
        targets.reshape(NB, BLK),
        stream_in.reshape(NB, NS, SUB, feat),
        layer_delta.reshape(NB, NS, SUB, feat),
        out_embed.reshape(NT, NC * LANE, VPART),
    )


def solution(mesh):
    placed = (
        P(None, "tp"),
        P("section", None, "tp"),
        P("tp"),
        P(None, "tp"),
        P("section", None),
        P("section"),
        P(),
    )
    return jax.shard_map(
        body, mesh=mesh, in_specs=placed, out_specs=P("section", None, None), check_vma=False
    )
```

```python
import functools
import heapq
import itertools

import jax
import jax.numpy as jnp
from jax import lax
from jax.experimental import pallas as pl
from jax.experimental.pallas import tpu as pltpu
from jax.sharding import PartitionSpec as P

BLK = 128
MAXB = 4
EPS = 1e-05
NS = 8
TX = 4
TZ = 4
NT = TX * TZ
SUB = BLK // NS
NPAIR = 2 * NS
NB = 4
NG = NPAIR - 1 + NB
ROWS = NG * SUB
LANE = 128
NC = 4
WIDTH = LANE * NC * NT
VPART = 1024
NTILE = 1024
DOWN = 2.0 ** -58
UP = 2.0 ** 58
F32 = jnp.float32
MESH = pl.DeviceIdType.MESH
ORDER = (0, 2, 3, 1)
HOP, LAND, GAP, DOT, DEPTH = 1.68, 2.2, 1.3, 0.33, 1


def long_sign(c):
    return 1 if c % 2 == 0 else -1


def rel_of(c, a, b):
    dx, dz = (a, b) if c < NC // 2 else (b, a)
    return (dx % TX) * TZ + dz % TZ


def step_of(c, axis, sign):
    along_x = (axis == 0) == (c < NC // 2)
    return (sign, 0) if along_x else (0, sign)


def forwards(c, a, b):
    go = long_sign(c)
    if (a, b) == (0, 0):
        return [(0, go), (0, -go), (1, go), (1, -go)]
    if b == 0:
        out = [(0, go)] if a == -go else []
        return out + [(1, go), (1, -go)]
    return [(1, go)] if b == -go else []


def wrap(v):
    v = v % 4
    return v - 4 if v == 3 else v


def ahead(c, a, b):
    return max([1 + ahead(c, *moved(a, b, axis, sign)) for axis, sign in forwards(c, a, b)], default=0)


def moved(a, b, axis, sign):
    return (wrap(a - sign), b) if axis == 0 else (a, wrap(b - sign))


def plan():
    tick = itertools.count()
    heap = [(GAP * i, 0, next(tick), ("own", c, 0, 0)) for i, c in enumerate(ORDER)]
    pending, loaded, free, ready = {}, {}, {}, {}
    steps, dots = [], []

    def feed(hop, now):
        queue = pending.get(hop, [])
        while queue and loaded.get(hop, 0) <= DEPTH:
            queue.sort()
            _, _, _, c, a, b, axis, sign = queue.pop(0)
            free[hop] = max(now, free.get(hop, 0.0)) + HOP
            loaded[hop] = loaded.get(hop, 0) + 1
            steps.append(("send", c, a, b, axis, sign))
            heapq.heappush(heap, (free[hop], 2, next(tick), ("free", hop)))
            landed = ("wait", c) + moved(a, b, axis, sign)
            heapq.heappush(heap, (free[hop] + LAND, 1, next(tick), landed))

    now = 0.0
    while heap:
        at, _, _, event = heapq.heappop(heap)
        now = max(now, at)
        if event[0] == "free":
            loaded[event[1]] -= 1
            feed(event[1], at)
            continue
        steps.append(event)
        _, c, a, b = event
        for axis, sign in forwards(c, a, b):
            hop = step_of(c, axis, sign)
            rank = (-ahead(c, *moved(a, b, axis, sign)), ORDER.index(c), next(tick))
            pending.setdefault(hop, []).append(rank + (c, a, b, axis, sign))
        for axis, sign in forwards(c, a, b):
            feed(step_of(c, axis, sign), now)
        key = (rel_of(c, a, b), c // 2)
        ready[key] = ready.get(key, 0) + 1
        if ready[key] == 2:
            dots.append(("dot",) + key)
        if dots and event[0] == "wait":
            steps.append(dots.pop(0))
            now += DOT
    return steps + dots


STEPS = plan()
FIRST_USE = list(dict.fromkeys(s[1] for s in STEPS if s[0] == "dot"))


FAR_FIRST = sorted(range(1, NT), key=lambda k: -abs(wrap(k // TZ)) - abs(wrap(k % TZ)))


def kernel(
    eb_hbm, ec_hbm, gain_hbm, tgt_hbm, stream_hbm, delta_hbm, w_hbm, out_ref,
    eb_s, ec_s, meta_s, own_s, blk_s, grp_s,
    gain_v, tgt_v, stream_v, delta_v, abuf, hid, sq, gath, wv, acc,
    ss_x, ss_z, scale_v, prob_v, tstat, tcol, pst, stat_v, loss_y, tot_v,
    loc_sem, w_sem, meta_send, meta_recv, a_send, a_recv, g_send, g_recv, ex_send, ex_recv, st_send, st_recv, y_send, y_recv,
):
    sec = lax.axis_index("section")
    tp = lax.axis_index("tp")
    px, pz = tp // TZ, tp % TZ

    def plane(dx, dz):
        return (sec, ((px + dx) % TX) * TZ + (pz + dz) % TZ)

    sec_peers = [((sec + k) % NS, tp) for k in (4, 3, 5, 2, 6, 1, 7)]
    x_peers = [plane(k, 0) for k in range(1, TX)]
    z_peers = [plane(0, k) for k in range(1, TZ)]
    tp_peers = [plane(k // TZ, k % TZ) for k in FAR_FIRST]
    everyone = sec_peers + [plane(1, 0), plane(-1, 0), plane(0, 1), plane(0, -1)]

    barrier = pltpu.get_barrier_semaphore()
    for peer in everyone:
        pl.semaphore_signal(barrier, inc=1, device_id=peer, device_id_type=MESH)

    local = [
        pltpu.make_async_copy(eb_hbm, eb_s, loc_sem.at[0]),
        pltpu.make_async_copy(ec_hbm, ec_s, loc_sem.at[1]),
        pltpu.make_async_copy(stream_hbm.at[:, sec], stream_v, loc_sem.at[2]),
        pltpu.make_async_copy(gain_hbm, gain_v, loc_sem.at[3]),
        pltpu.make_async_copy(tgt_hbm, tgt_v, loc_sem.at[4]),
    ]
    own_delta = [
        pltpu.make_async_copy(
            delta_hbm.at[:, sec, :, pl.ds(c * LANE, LANE)], abuf.at[c, sec], loc_sem.at[5 + c]
        )
        for c in range(NC)
    ]
    all_delta = pltpu.make_async_copy(delta_hbm, delta_v, loc_sem.at[10])
    for copy in local[:2] + [all_delta] + local[2:] + own_delta:
        copy.start()

    local[0].wait()
    local[1].wait()
    for k in range(MAXB):
        meta_s[sec, 0, k] = eb_s[0, k]
    meta_s[sec, 0, MAXB] = ec_s[0, 0]

    all_delta.wait()
    pl.semaphore_wait(barrier, len(everyone))

    sends = []

    def send(src, dst, send_sem, recv_sem, peer):
        copy = pltpu.make_async_remote_copy(
            src_ref=src, dst_ref=dst, send_sem=send_sem, recv_sem=recv_sem,
            device_id=peer, device_id_type=MESH,
        )
        copy.start()
        sends.append(copy)

    def arrived(dst, recv_sem, any_sem):
        pltpu.make_async_remote_copy(
            src_ref=dst, dst_ref=dst, send_sem=any_sem, recv_sem=recv_sem,
            device_id=x_peers[0], device_id_type=MESH,
        ).wait_recv()

    for k, peer in enumerate(sec_peers):
        send(meta_s.at[sec], meta_s.at[sec], meta_send.at[k], meta_recv.at[sec], peer)
    for c in ORDER:
        for k, peer in enumerate(sec_peers):
            send(
                delta_v.at[:, peer[0], :, pl.ds(c * LANE, LANE)], abuf.at[c, sec],
                a_send.at[c, k], a_recv.at[c, sec], peer,
            )

    w_copies = {}
    for i, rel in enumerate(FIRST_USE):
        src_tp = ((px + rel // TZ) % TX) * TZ + (pz + rel % TZ) % TZ
        w_copies[rel] = pltpu.make_async_copy(w_hbm.at[src_tp], wv.at[rel], w_sem.at[i])
        w_copies[rel].start()

    for peer in sec_peers:
        arrived(meta_s.at[peer[0]], meta_recv.at[peer[0]], meta_send.at[0])
    counts = [meta_s[u, 0, MAXB] for u in range(NS)]
    offs = [jnp.int32(0)]
    for u in range(NS - 1):
        offs.append(offs[-1] + counts[u])
    for j in range(NPAIR):
        owner = jnp.int32(0)
        base = jnp.int32(0)
        for u in range(1, NS):
            owner = jnp.where(offs[u] <= j, u, owner)
            base = jnp.where(offs[u] <= j, offs[u], base)
        block = meta_s[owner, 0, jnp.minimum(j - base, MAXB - 1)]
        own_s[j] = owner
        blk_s[j] = block
        grp_s[j] = j if j < NPAIR - 1 else NPAIR - 1 + block

    local[2].wait()
    local[3].wait()
    local[4].wait()
    lane_r = lax.broadcasted_iota(jnp.int32, (SUB, LANE), 1)
    sub_r = lax.broadcasted_iota(jnp.int32, (SUB, LANE), 0)
    mine = lane_r == sec * SUB + sub_r
    for b in range(NB):
        row = jnp.broadcast_to(tgt_v[b : b + 1, :].astype(F32), (SUB, LANE))
        col = jnp.sum(jnp.where(mine, row, 0.0), axis=1, keepdims=True)
        tcol[b] = jnp.broadcast_to(col, (SUB, LANE)) - (tp * VPART).astype(F32)

    hop = itertools.count()

    def pass_on(c, a, b, axis, sign):
        there = rel_of(c, *moved(a, b, axis, sign))
        send(
            gath.at[rel_of(c, a, b), c], gath.at[there, c],
            g_send.at[next(hop)], g_recv.at[there, c],
            plane(*step_of(c, axis, sign)),
        )

    def own_shard(c):
        own_delta[c].wait()
        for peer in sec_peers:
            arrived(abuf.at[c, peer[0]], a_recv.at[c, peer[0]], a_send.at[0, 0])
        state = stream_v[:, :, pl.ds(c * LANE, LANE)].astype(F32)
        for u in range(NS):
            state = state + abuf[c, u].astype(F32)
            hid[u] = state
        gain = gain_v[c : c + 1, :] * DOWN

        def put(g, rows):
            sq[g] = rows * rows if c == ORDER[0] else sq[g] + rows * rows
            gath[0, c, pl.ds(g * SUB, SUB), :] = (rows * gain).astype(jnp.bfloat16)

        for j in range(NPAIR - 1):
            put(j, hid[own_s[j], blk_s[j]])
        for b in range(NB):
            put(NPAIR - 1 + b, hid[NS - 1, b])

    def share(buf, place, peers, stage):
        for k, peer in enumerate(peers):
            send(buf.at[place], buf.at[place], ex_send.at[stage, k], ex_recv.at[stage, place], peer)

    def collect(buf, place, stage):
        for k in range(1, 4):
            there = (place + k) % 4
            arrived(buf.at[there], ex_recv.at[stage, there], ex_send.at[stage, 0])

    def squares():
        for g in range(NG, 24):
            sq[g] = jnp.zeros((SUB, LANE), F32)
        sums = []
        for q in range(3):
            part = sq[pl.ds(q * 8, 8)].reshape(LANE, LANE)
            sums.append(jnp.sum(part.T, axis=0, keepdims=True))
        ss_x[px] = jnp.concatenate(sums + [jnp.zeros((5, LANE), F32)], axis=0)
        share(ss_x, px, x_peers, 0)

    seen = set()
    waits = owns = 0
    for step in STEPS:
        if step[0] == "own":
            own_shard(step[1])
            owns += 1
            first_wait = waits
        elif step[0] == "send":
            pass_on(*step[1:])
        elif step[0] == "wait":
            _, c, a, b = step
            rel = rel_of(c, a, b)
            arrived(gath.at[rel, c], g_recv.at[rel, c], g_send.at[0])
            waits += 1
            if owns == NC and waits == first_wait + 1:
                squares()
            if owns == NC and waits == first_wait + 10:
                collect(ss_x, px, 0)
                ss_z[pz] = ss_x[0] + ss_x[1] + ss_x[2] + ss_x[3]
                share(ss_z, pz, z_peers, 1)
            if owns == NC and waits == first_wait + 24:
                collect(ss_z, pz, 1)
                total = ss_z[0] + ss_z[1] + ss_z[2] + ss_z[3]
                scale = lax.rsqrt(total / WIDTH + EPS) * UP
                for q in range(3):
                    wide = jnp.broadcast_to(scale[q : q + 1, :], (LANE, LANE)).T
                    scale_v[pl.ds(q * 8, 8)] = wide.reshape(8, SUB, LANE)
        else:
            _, rel, half = step
            if rel not in seen:
                w_copies[rel].wait()
            first = not seen
            seen.add(rel)

            def tile(n, carry, rel=rel, half=half, first=first):
                cols = pl.ds(pl.multiple_of(n * NTILE, NTILE), NTILE)
                lhs = jnp.concatenate([gath[rel, 2 * half], gath[rel, 2 * half + 1]], axis=1)
                rhs = wv[rel, pl.ds(half * 2 * LANE, 2 * LANE), cols]
                part = jnp.dot(lhs, rhs, preferred_element_type=F32).reshape(NG, SUB, NTILE)
                acc[:, :, cols] = part if first else acc[:, :, cols] + part
                return carry

            lax.fori_loop(0, VPART // NTILE, tile, 0)

    def wide8(v):
        return jnp.concatenate([v] * (VPART // LANE), axis=1)

    def teach(b, carry):
        logit = acc[NPAIR - 1 + b] * wide8(scale_v[NPAIR - 1 + b])
        peak = jnp.max(logit, axis=1, keepdims=True)
        weight = jnp.exp(logit - peak)
        prob_v[b] = weight
        total = jnp.sum(weight, axis=1, keepdims=True)
        tstat[b] = jnp.where(lane_r == 2, peak, jnp.where(lane_r == 3, total, 0.0))
        return carry

    lax.fori_loop(0, NB, teach, 0, unroll=True)
    column = lax.broadcasted_iota(jnp.int32, (SUB, VPART), 1).astype(F32)

    def leave(j, carry):
        block = blk_s[j]
        group = grp_s[j]
        exit_logit = acc[group] * wide8(scale_v[group])
        teach_logit = acc[NPAIR - 1 + block] * wide8(scale_v[NPAIR - 1 + block])
        weight = prob_v[block]
        peak = jnp.max(exit_logit, axis=1, keepdims=True)
        total = jnp.sum(jnp.exp(exit_logit - peak), axis=1, keepdims=True)
        cross = jnp.sum(weight * (teach_logit - exit_logit), axis=1, keepdims=True)
        hit = wide8(tcol[block]) == column
        picked = jnp.sum(jnp.where(hit, exit_logit, 0.0), axis=1, keepdims=True)
        out = tstat[block]
        for k, v in ((0, peak), (1, total), (4, cross), (5, picked)):
            out = jnp.where(lane_r == k, v, out)
        pst[j] = out
        return carry

    lax.fori_loop(0, NPAIR, leave, 0, unroll=8)
    halves = []
    for q in range(2):
        st = pst[pl.ds(q * 8, 8)].reshape(LANE, LANE).T
        lse_e = st[0:1, :] + jnp.log(st[1:2, :])
        lse_t = st[2:3, :] + jnp.log(st[3:4, :])
        halves += [lse_e, lse_t, st[4:5, :] / st[3:4, :], st[5:6, :]]
    stat_v[tp] = jnp.concatenate(halves, axis=0)
    for k, (_, there) in enumerate(tp_peers):
        send(stat_v.at[tp], stat_v.at[tp], st_send.at[k], st_recv.at[tp], (sec, there))
    for _, there in tp_peers:
        arrived(stat_v.at[there], st_recv.at[there], st_send.at[0])
    parts = [stat_v[i] for i in range(NT)]
    peak = functools.reduce(jnp.maximum, parts)
    mass = picked = cross = 0.0
    for p in parts:
        share_of = jnp.exp(p - peak)
        mass = mass + share_of
        cross = cross + pltpu.roll(share_of, 1, 0) * p
        picked = picked + p
    lse = peak + jnp.log(mass)
    loss = jnp.concatenate(
        [
            2.0 * lse[q : q + 1] - picked[q + 3 : q + 4] + cross[q + 2 : q + 3] / mass[q + 1 : q + 2] - lse[q + 1 : q + 2]
            for q in (0, 4)
        ],
        axis=1,
    )

    at = lax.broadcasted_iota(jnp.int32, (NPAIR, NPAIR * SUB), 1) // SUB
    pair = lax.broadcasted_iota(jnp.int32, (NPAIR, NPAIR * SUB), 0)
    spread = jnp.where(at == pair, jnp.broadcast_to(loss, (NPAIR, NPAIR * SUB)), 0.0)
    spread = spread[:, :LANE] + spread[:, LANE:]
    for shift in (64, 32, 16):
        spread = spread + pltpu.roll(spread, shift, 1)
    place = lax.broadcasted_iota(jnp.int32, (NPAIR, LANE), 1) // SUB
    low, high = spread[: NPAIR // 2], spread[NPAIR // 2 :]
    place = place[: NPAIR // 2]
    loss_y[sec] = jnp.where(place == 0, low, jnp.where(place == 1, high, 0.0))
    for k, peer in enumerate(sec_peers):
        send(loss_y.at[sec], loss_y.at[sec], y_send.at[k], y_recv.at[sec], peer)
    for peer in sec_peers:
        arrived(loss_y.at[peer[0]], y_recv.at[peer[0]], y_send.at[0])
    low = high = jnp.zeros((NPAIR // 2, LANE), F32)
    for u in range(NS):
        low = jnp.where(place == u, pltpu.roll(loss_y[u], SUB * u, 1), low)
        high = jnp.where(place == u, pltpu.roll(loss_y[u], (SUB * (u - 1)) % LANE, 1), high)
    tot_v[pl.ds(0, NPAIR // 2)] = low
    tot_v[pl.ds(NPAIR // 2, NPAIR // 2)] = high
    tot_v[pl.ds(NPAIR, 8)] = jnp.zeros((8, LANE), F32)
    start = jnp.int32(0)
    for u in range(NS):
        start = start + jnp.where(u < sec, counts[u], 0)
    for k in range(MAXB):
        row = tot_v[pl.ds(start + k, 1), :]
        out_ref[0, pl.ds(k, 1), :] = jnp.where(k < ec_s[0, 0], row, 0.0)
    for copy in sends:
        copy.wait_send()


def body(stream_in, layer_delta, norm_gain, out_embed, exit_blocks, exit_counts, targets):
    feat = stream_in.shape[1]
    any_spec = pl.BlockSpec(memory_space=pl.ANY)
    dma = pltpu.SemaphoreType.DMA
    bf16, i32 = jnp.bfloat16, jnp.int32
    vm = pltpu.VMEM
    return pl.pallas_call(
        kernel,
        out_shape=jax.ShapeDtypeStruct((1, MAXB, BLK), F32),
        in_specs=[any_spec] * 7,
        out_specs=pl.BlockSpec(memory_space=pltpu.VMEM),
        scratch_shapes=[
            pltpu.SMEM((1, MAXB), i32),
            pltpu.SMEM((1, 1), i32),
            pltpu.SMEM((NS, 1, LANE), i32),
            pltpu.SMEM((NPAIR,), i32),
            pltpu.SMEM((NPAIR,), i32),
            pltpu.SMEM((NPAIR,), i32),
            vm((NC, LANE), F32),
            vm((NB, BLK), i32),
            vm((NB, SUB, feat), bf16),
            vm((NB, NS, SUB, feat), bf16),
            vm((NC, NS, NB, SUB, LANE), bf16),
            vm((NS, NB, SUB, LANE), F32),
            vm((24, SUB, LANE), F32),
            vm((NT, NC, ROWS, LANE), bf16),
            vm((NT, NC * LANE, VPART), bf16),
            vm((NG, SUB, VPART), F32),
            vm((TX, 8, LANE), F32),
            vm((TZ, 8, LANE), F32),
            vm((24, SUB, LANE), F32),
            vm((NB, SUB, VPART), F32),
            vm((NB, SUB, LANE), F32),
            vm((NB, SUB, LANE), F32),
            vm((NPAIR, SUB, LANE), F32),
            vm((NT, 8, LANE), F32),
            vm((NS, NPAIR // 2, LANE), F32),
            vm((24, LANE), F32),
            dma((11,)),
            dma((NT,)),
            dma((NS - 1,)),
            dma((NS,)),
            dma((NC, NS - 1)),
            dma((NC, NS)),
            dma((NC * (NT - 1),)),
            dma((NT, NC)),
            dma((2, 3)),
            dma((2, 4)),
            dma((NT - 1,)),
            dma((NT,)),
            dma((NS - 1,)),
            dma((NS,)),
        ],
        compiler_params=pltpu.CompilerParams(
            collective_id=0, has_side_effects=True, vmem_limit_bytes=48 * 1024 * 1024
        ),
    )(
        pltpu.with_memory_space_constraint(exit_blocks, pltpu.HBM),
        exit_counts.reshape(1, 1),
        pltpu.with_memory_space_constraint(norm_gain.reshape(NC, LANE), pltpu.HBM),
        pltpu.with_memory_space_constraint(targets.reshape(NB, BLK), pltpu.HBM),
        pltpu.with_memory_space_constraint(stream_in.reshape(NB, NS, SUB, feat), pltpu.HBM),
        pltpu.with_memory_space_constraint(layer_delta.reshape(NB, NS, SUB, feat), pltpu.HBM),
        out_embed.reshape(NT, NC * LANE, VPART),
    )


def solution(mesh):
    placed = (
        P(None, "tp"),
        P("section", None, "tp"),
        P("tp"),
        P(None, "tp"),
        P("section", None),
        P("section"),
        P(),
    )
    return jax.shard_map(
        body, mesh=mesh, in_specs=placed, out_specs=P("section", None, None), check_vma=False
    )
```

```python
import functools
import heapq
import itertools

import jax
import jax.numpy as jnp
from jax import lax
from jax.experimental import pallas as pl
from jax.experimental.pallas import tpu as pltpu
from jax.sharding import PartitionSpec as P

BLK = 128
MAXB = 4
EPS = 1e-05
NS = 8
TX = 4
TZ = 4
NT = TX * TZ
SUB = BLK // NS
NPAIR = 2 * NS
NB = 4
NG = NPAIR - 1 + NB
ROWS = NG * SUB
LANE = 128
NC = 4
WIDTH = LANE * NC * NT
VPART = 1024
NTILE = 1024
DOWN = 2.0 ** -58
UP = 2.0 ** 58
F32 = jnp.float32
MESH = pl.DeviceIdType.MESH
ORDER = (0, 2, 3, 1)
HOP, LAND, GAP, DOT, DEPTH = 1.68, 2.2, 1.3, 0.33, 1


def long_sign(c):
    return 1 if c % 2 == 0 else -1


def rel_of(c, a, b):
    dx, dz = (a, b) if c < NC // 2 else (b, a)
    return (dx % TX) * TZ + dz % TZ


def step_of(c, axis, sign):
    along_x = (axis == 0) == (c < NC // 2)
    return (sign, 0) if along_x else (0, sign)


def forwards(c, a, b):
    go = long_sign(c)
    if (a, b) == (0, 0):
        return [(0, go), (0, -go), (1, go), (1, -go)]
    if b == 0:
        out = [(0, go)] if a == -go else []
        return out + [(1, go), (1, -go)]
    return [(1, go)] if b == -go else []


def wrap(v):
    v = v % 4
    return v - 4 if v == 3 else v


def ahead(c, a, b):
    return max([1 + ahead(c, *moved(a, b, axis, sign)) for axis, sign in forwards(c, a, b)], default=0)


def moved(a, b, axis, sign):
    return (wrap(a - sign), b) if axis == 0 else (a, wrap(b - sign))


def plan():
    tick = itertools.count()
    heap = [(GAP * i, 0, next(tick), ("own", c, 0, 0)) for i, c in enumerate(ORDER)]
    pending, loaded, free, ready = {}, {}, {}, {}
    steps, dots = [], []

    def feed(hop, now):
        queue = pending.get(hop, [])
        while queue and loaded.get(hop, 0) <= DEPTH:
            queue.sort()
            _, _, _, c, a, b, axis, sign = queue.pop(0)
            free[hop] = max(now, free.get(hop, 0.0)) + HOP
            loaded[hop] = loaded.get(hop, 0) + 1
            steps.append(("send", c, a, b, axis, sign))
            heapq.heappush(heap, (free[hop], 2, next(tick), ("free", hop)))
            landed = ("wait", c) + moved(a, b, axis, sign)
            heapq.heappush(heap, (free[hop] + LAND, 1, next(tick), landed))

    now = 0.0
    while heap:
        at, _, _, event = heapq.heappop(heap)
        now = max(now, at)
        if event[0] == "free":
            loaded[event[1]] -= 1
            feed(event[1], at)
            continue
        steps.append(event)
        _, c, a, b = event
        for axis, sign in forwards(c, a, b):
            hop = step_of(c, axis, sign)
            rank = (-ahead(c, *moved(a, b, axis, sign)), ORDER.index(c), next(tick))
            pending.setdefault(hop, []).append(rank + (c, a, b, axis, sign))
        for axis, sign in forwards(c, a, b):
            feed(step_of(c, axis, sign), now)
        key = (rel_of(c, a, b), c // 2)
        ready[key] = ready.get(key, 0) + 1
        if ready[key] == 2:
            dots.append(("dot",) + key)
        if dots and event[0] == "wait":
            steps.append(dots.pop(0))
            now += DOT
    return steps + dots


STEPS = plan()
FIRST_USE = list(dict.fromkeys(s[1] for s in STEPS if s[0] == "dot"))


FAR_FIRST = sorted(range(1, NT), key=lambda k: -abs(wrap(k // TZ)) - abs(wrap(k % TZ)))


def kernel(
    eb_hbm, ec_hbm, gain_hbm, tgt_hbm, stream_hbm, delta_hbm, w_hbm, out_ref,
    eb_s, ec_s, meta_s, own_s, blk_s, grp_s,
    gain_v, tgt_v, stream_v, delta_v, abuf, hid, sq, gath, wv, acc,
    ss_x, ss_z, scale_v, prob_v, tstat, tcol, pst, stat_v, loss_y, tot_v,
    loc_sem, w_sem, meta_send, meta_recv, a_send, a_recv, g_send, g_recv, ex_send, ex_recv, st_send, st_recv, y_send, y_recv,
):
    sec = lax.axis_index("section")
    tp = lax.axis_index("tp")
    px, pz = tp // TZ, tp % TZ

    def plane(dx, dz):
        return (sec, ((px + dx) % TX) * TZ + (pz + dz) % TZ)

    sec_peers = [((sec + k) % NS, tp) for k in (4, 3, 5, 2, 6, 1, 7)]
    x_peers = [plane(k, 0) for k in range(1, TX)]
    z_peers = [plane(0, k) for k in range(1, TZ)]
    tp_peers = [plane(k // TZ, k % TZ) for k in FAR_FIRST]
    everyone = sec_peers + [plane(1, 0), plane(-1, 0), plane(0, 1), plane(0, -1)]

    barrier = pltpu.get_barrier_semaphore()
    for peer in everyone:
        pl.semaphore_signal(barrier, inc=1, device_id=peer, device_id_type=MESH)

    local = [
        pltpu.make_async_copy(eb_hbm, eb_s, loc_sem.at[0]),
        pltpu.make_async_copy(ec_hbm, ec_s, loc_sem.at[1]),
        pltpu.make_async_copy(stream_hbm.at[:, sec], stream_v, loc_sem.at[2]),
        pltpu.make_async_copy(gain_hbm, gain_v, loc_sem.at[3]),
        pltpu.make_async_copy(tgt_hbm, tgt_v, loc_sem.at[4]),
    ]
    own_delta = [
        pltpu.make_async_copy(
            delta_hbm.at[:, sec, :, pl.ds(c * LANE, LANE)], abuf.at[c, sec], loc_sem.at[5 + c]
        )
        for c in range(NC)
    ]
    all_delta = pltpu.make_async_copy(delta_hbm, delta_v, loc_sem.at[10])
    for copy in local[:2] + [all_delta] + local[2:] + own_delta:
        copy.start()

    local[0].wait()
    local[1].wait()
    for k in range(MAXB):
        meta_s[sec, 0, k] = eb_s[0, k]
    meta_s[sec, 0, MAXB] = ec_s[0, 0]

    all_delta.wait()
    pl.semaphore_wait(barrier, len(everyone))

    sends = []

    def send(src, dst, send_sem, recv_sem, peer):
        copy = pltpu.make_async_remote_copy(
            src_ref=src, dst_ref=dst, send_sem=send_sem, recv_sem=recv_sem,
            device_id=peer, device_id_type=MESH,
        )
        copy.start()
        sends.append(copy)

    def arrived(dst, recv_sem, any_sem):
        pltpu.make_async_remote_copy(
            src_ref=dst, dst_ref=dst, send_sem=any_sem, recv_sem=recv_sem,
            device_id=x_peers[0], device_id_type=MESH,
        ).wait_recv()

    for k, peer in enumerate(sec_peers):
        send(meta_s.at[sec], meta_s.at[sec], meta_send.at[k], meta_recv.at[sec], peer)
    for c in ORDER:
        for k, peer in enumerate(sec_peers):
            send(
                delta_v.at[:, peer[0], :, pl.ds(c * LANE, LANE)], abuf.at[c, sec],
                a_send.at[c, k], a_recv.at[c, sec], peer,
            )

    w_copies = {}
    for i, rel in enumerate(FIRST_USE):
        src_tp = ((px + rel // TZ) % TX) * TZ + (pz + rel % TZ) % TZ
        w_copies[rel] = pltpu.make_async_copy(w_hbm.at[src_tp], wv.at[rel], w_sem.at[i])
        w_copies[rel].start()

    for peer in sec_peers:
        arrived(meta_s.at[peer[0]], meta_recv.at[peer[0]], meta_send.at[0])
    counts = [meta_s[u, 0, MAXB] for u in range(NS)]
    offs = [jnp.int32(0)]
    for u in range(NS - 1):
        offs.append(offs[-1] + counts[u])
    for j in range(NPAIR):
        owner = jnp.int32(0)
        base = jnp.int32(0)
        for u in range(1, NS):
            owner = jnp.where(offs[u] <= j, u, owner)
            base = jnp.where(offs[u] <= j, offs[u], base)
        block = meta_s[owner, 0, jnp.minimum(j - base, MAXB - 1)]
        own_s[j] = owner
        blk_s[j] = block
        grp_s[j] = j if j < NPAIR - 1 else NPAIR - 1 + block

    local[2].wait()
    local[3].wait()
    local[4].wait()
    lane_r = lax.broadcasted_iota(jnp.int32, (SUB, LANE), 1)
    sub_r = lax.broadcasted_iota(jnp.int32, (SUB, LANE), 0)
    mine = lane_r == sec * SUB + sub_r
    for b in range(NB):
        row = jnp.broadcast_to(tgt_v[b : b + 1, :].astype(F32), (SUB, LANE))
        col = jnp.sum(jnp.where(mine, row, 0.0), axis=1, keepdims=True)
        tcol[b] = jnp.broadcast_to(col, (SUB, LANE)) - (tp * VPART).astype(F32)

    hop = itertools.count()

    def pass_on(c, a, b, axis, sign):
        there = rel_of(c, *moved(a, b, axis, sign))
        send(
            gath.at[rel_of(c, a, b), c], gath.at[there, c],
            g_send.at[next(hop)], g_recv.at[there, c],
            plane(*step_of(c, axis, sign)),
        )

    def own_shard(c):
        own_delta[c].wait()
        for peer in sec_peers:
            arrived(abuf.at[c, peer[0]], a_recv.at[c, peer[0]], a_send.at[0, 0])
        state = stream_v[:, :, pl.ds(c * LANE, LANE)].astype(F32)
        for u in range(NS):
            state = state + abuf[c, u].astype(F32)
            hid[u] = state
        gain = gain_v[c : c + 1, :] * DOWN

        def put(g, rows):
            sq[g] = rows * rows if c == ORDER[0] else sq[g] + rows * rows
            gath[0, c, pl.ds(g * SUB, SUB), :] = (rows * gain).astype(jnp.bfloat16)

        for j in range(NPAIR - 1):
            put(j, hid[own_s[j], blk_s[j]])
        for b in range(NB):
            put(NPAIR - 1 + b, hid[NS - 1, b])

    def share(buf, place, peers, stage):
        for k, peer in enumerate(peers):
            send(buf.at[place], buf.at[place], ex_send.at[stage, k], ex_recv.at[stage, place], peer)

    def collect(buf, place, stage):
        for k in range(1, 4):
            there = (place + k) % 4
            arrived(buf.at[there], ex_recv.at[stage, there], ex_send.at[stage, 0])

    def squares():
        for g in range(NG, 24):
            sq[g] = jnp.zeros((SUB, LANE), F32)
        sums = []
        for q in range(3):
            part = sq[pl.ds(q * 8, 8)].reshape(LANE, LANE)
            sums.append(jnp.sum(part.T, axis=0, keepdims=True))
        ss_x[px] = jnp.concatenate(sums + [jnp.zeros((5, LANE), F32)], axis=0)
        share(ss_x, px, x_peers, 0)

    seen = set()
    waits = owns = 0
    for step in STEPS:
        if step[0] == "own":
            own_shard(step[1])
            owns += 1
            first_wait = waits
        elif step[0] == "send":
            pass_on(*step[1:])
        elif step[0] == "wait":
            _, c, a, b = step
            rel = rel_of(c, a, b)
            arrived(gath.at[rel, c], g_recv.at[rel, c], g_send.at[0])
            waits += 1
            if owns == NC and waits == first_wait + 1:
                squares()
            if owns == NC and waits == first_wait + 10:
                collect(ss_x, px, 0)
                ss_z[pz] = ss_x[0] + ss_x[1] + ss_x[2] + ss_x[3]
                share(ss_z, pz, z_peers, 1)
            if owns == NC and waits == first_wait + 24:
                collect(ss_z, pz, 1)
                total = ss_z[0] + ss_z[1] + ss_z[2] + ss_z[3]
                scale = lax.rsqrt(total / WIDTH + EPS) * UP
                for q in range(3):
                    wide = jnp.broadcast_to(scale[q : q + 1, :], (LANE, LANE)).T
                    scale_v[pl.ds(q * 8, 8)] = wide.reshape(8, SUB, LANE)
        else:
            _, rel, half = step
            if rel not in seen:
                w_copies[rel].wait()
            first = not seen
            seen.add(rel)

            def tile(n, carry, rel=rel, half=half, first=first):
                cols = pl.ds(pl.multiple_of(n * NTILE, NTILE), NTILE)
                lhs = jnp.concatenate([gath[rel, 2 * half], gath[rel, 2 * half + 1]], axis=1)
                rhs = wv[rel, pl.ds(half * 2 * LANE, 2 * LANE), cols]
                part = jnp.dot(lhs, rhs, preferred_element_type=F32).reshape(NG, SUB, NTILE)
                acc[:, :, cols] = part if first else acc[:, :, cols] + part
                return carry

            lax.fori_loop(0, VPART // NTILE, tile, 0)

    def wide8(v):
        return jnp.concatenate([v] * (VPART // LANE), axis=1)

    def teach(b, carry):
        logit = acc[NPAIR - 1 + b] * wide8(scale_v[NPAIR - 1 + b])
        peak = jnp.max(logit, axis=1, keepdims=True)
        weight = jnp.exp(logit - peak)
        prob_v[b] = weight
        total = jnp.sum(weight, axis=1, keepdims=True)
        tstat[b] = jnp.where(lane_r == 2, peak, jnp.where(lane_r == 3, total, 0.0))
        return carry

    lax.fori_loop(0, NB, teach, 0, unroll=True)
    column = lax.broadcasted_iota(jnp.int32, (SUB, VPART), 1).astype(F32)

    def leave(j, carry):
        block = blk_s[j]
        group = grp_s[j]
        exit_logit = acc[group] * wide8(scale_v[group])
        teach_logit = acc[NPAIR - 1 + block] * wide8(scale_v[NPAIR - 1 + block])
        weight = prob_v[block]
        peak = jnp.max(exit_logit, axis=1, keepdims=True)
        total = jnp.sum(jnp.exp(exit_logit - peak), axis=1, keepdims=True)
        cross = jnp.sum(weight * (teach_logit - exit_logit), axis=1, keepdims=True)
        hit = wide8(tcol[block]) == column
        picked = jnp.sum(jnp.where(hit, exit_logit, 0.0), axis=1, keepdims=True)
        out = tstat[block]
        for k, v in ((0, peak), (1, total), (4, cross), (5, picked)):
            out = jnp.where(lane_r == k, v, out)
        pst[j] = out
        return carry

    lax.fori_loop(0, NPAIR, leave, 0, unroll=True)
    halves = []
    for q in range(2):
        st = pst[pl.ds(q * 8, 8)].reshape(LANE, LANE).T
        lse_e = st[0:1, :] + jnp.log(st[1:2, :])
        lse_t = st[2:3, :] + jnp.log(st[3:4, :])
        halves += [lse_e, lse_t, st[4:5, :] / st[3:4, :], st[5:6, :]]
    stat_v[tp] = jnp.concatenate(halves, axis=0)
    early = list(sends)
    sends.clear()
    for k, (_, there) in enumerate(tp_peers):
        send(stat_v.at[tp], stat_v.at[tp], st_send.at[k], st_recv.at[tp], (sec, there))
    for copy in early:
        copy.wait_send()
    for _, there in tp_peers:
        arrived(stat_v.at[there], st_recv.at[there], st_send.at[0])
    parts = [stat_v[i] for i in range(NT)]
    peak = functools.reduce(jnp.maximum, parts)
    mass = picked = cross = 0.0
    for p in parts:
        share_of = jnp.exp(p - peak)
        mass = mass + share_of
        cross = cross + pltpu.roll(share_of, 1, 0) * p
        picked = picked + p
    lse = peak + jnp.log(mass)
    loss = jnp.concatenate(
        [
            2.0 * lse[q : q + 1] - picked[q + 3 : q + 4] + cross[q + 2 : q + 3] / mass[q + 1 : q + 2] - lse[q + 1 : q + 2]
            for q in (0, 4)
        ],
        axis=1,
    )

    at = lax.broadcasted_iota(jnp.int32, (NPAIR, NPAIR * SUB), 1) // SUB
    pair = lax.broadcasted_iota(jnp.int32, (NPAIR, NPAIR * SUB), 0)
    spread = jnp.where(at == pair, jnp.broadcast_to(loss, (NPAIR, NPAIR * SUB)), 0.0)
    spread = spread[:, :LANE] + spread[:, LANE:]
    for shift in (64, 32, 16):
        spread = spread + pltpu.roll(spread, shift, 1)
    place = lax.broadcasted_iota(jnp.int32, (NPAIR, LANE), 1) // SUB
    low, high = spread[: NPAIR // 2], spread[NPAIR // 2 :]
    place = place[: NPAIR // 2]
    loss_y[sec] = jnp.where(place == 0, low, jnp.where(place == 1, high, 0.0))
    early = list(sends)
    sends.clear()
    for k, peer in enumerate(sec_peers):
        send(loss_y.at[sec], loss_y.at[sec], y_send.at[k], y_recv.at[sec], peer)
    for copy in early:
        copy.wait_send()
    for peer in sec_peers:
        arrived(loss_y.at[peer[0]], y_recv.at[peer[0]], y_send.at[0])
    low = high = jnp.zeros((NPAIR // 2, LANE), F32)
    for u in range(NS):
        low = jnp.where(place == u, pltpu.roll(loss_y[u], SUB * u, 1), low)
        high = jnp.where(place == u, pltpu.roll(loss_y[u], (SUB * (u - 1)) % LANE, 1), high)
    tot_v[pl.ds(0, NPAIR // 2)] = low
    tot_v[pl.ds(NPAIR // 2, NPAIR // 2)] = high
    tot_v[pl.ds(NPAIR, 8)] = jnp.zeros((8, LANE), F32)
    start = jnp.int32(0)
    for u in range(NS):
        start = start + jnp.where(u < sec, counts[u], 0)
    for k in range(MAXB):
        row = tot_v[pl.ds(start + k, 1), :]
        out_ref[0, pl.ds(k, 1), :] = jnp.where(k < ec_s[0, 0], row, 0.0)
    for copy in sends:
        copy.wait_send()


def body(stream_in, layer_delta, norm_gain, out_embed, exit_blocks, exit_counts, targets):
    feat = stream_in.shape[1]
    any_spec = pl.BlockSpec(memory_space=pl.ANY)
    dma = pltpu.SemaphoreType.DMA
    bf16, i32 = jnp.bfloat16, jnp.int32
    vm = pltpu.VMEM
    return pl.pallas_call(
        kernel,
        out_shape=jax.ShapeDtypeStruct((1, MAXB, BLK), F32),
        in_specs=[any_spec] * 7,
        out_specs=pl.BlockSpec(memory_space=pltpu.VMEM),
        scratch_shapes=[
            pltpu.SMEM((1, MAXB), i32),
            pltpu.SMEM((1, 1), i32),
            pltpu.SMEM((NS, 1, LANE), i32),
            pltpu.SMEM((NPAIR,), i32),
            pltpu.SMEM((NPAIR,), i32),
            pltpu.SMEM((NPAIR,), i32),
            vm((NC, LANE), F32),
            vm((NB, BLK), i32),
            vm((NB, SUB, feat), bf16),
            vm((NB, NS, SUB, feat), bf16),
            vm((NC, NS, NB, SUB, LANE), bf16),
            vm((NS, NB, SUB, LANE), F32),
            vm((24, SUB, LANE), F32),
            vm((NT, NC, ROWS, LANE), bf16),
            vm((NT, NC * LANE, VPART), bf16),
            vm((NG, SUB, VPART), F32),
            vm((TX, 8, LANE), F32),
            vm((TZ, 8, LANE), F32),
            vm((24, SUB, LANE), F32),
            vm((NB, SUB, VPART), F32),
            vm((NB, SUB, LANE), F32),
            vm((NB, SUB, LANE), F32),
            vm((NPAIR, SUB, LANE), F32),
            vm((NT, 8, LANE), F32),
            vm((NS, NPAIR // 2, LANE), F32),
            vm((24, LANE), F32),
            dma((11,)),
            dma((NT,)),
            dma((NS - 1,)),
            dma((NS,)),
            dma((NC, NS - 1)),
            dma((NC, NS)),
            dma((NC * (NT - 1),)),
            dma((NT, NC)),
            dma((2, 3)),
            dma((2, 4)),
            dma((NT - 1,)),
            dma((NT,)),
            dma((NS - 1,)),
            dma((NS,)),
        ],
        compiler_params=pltpu.CompilerParams(
            collective_id=0, has_side_effects=True, vmem_limit_bytes=48 * 1024 * 1024
        ),
    )(
        pltpu.with_memory_space_constraint(exit_blocks, pltpu.HBM),
        exit_counts.reshape(1, 1),
        pltpu.with_memory_space_constraint(norm_gain.reshape(NC, LANE), pltpu.HBM),
        pltpu.with_memory_space_constraint(targets.reshape(NB, BLK), pltpu.HBM),
        pltpu.with_memory_space_constraint(stream_in.reshape(NB, NS, SUB, feat), pltpu.HBM),
        pltpu.with_memory_space_constraint(layer_delta.reshape(NB, NS, SUB, feat), pltpu.HBM),
        out_embed.reshape(NT, NC * LANE, VPART),
    )


def solution(mesh):
    placed = (
        P(None, "tp"),
        P("section", None, "tp"),
        P("tp"),
        P(None, "tp"),
        P("section", None),
        P("section"),
        P(),
    )
    return jax.shard_map(
        body, mesh=mesh, in_specs=placed, out_specs=P("section", None, None), check_vma=False
    )
```

```python
import functools
import heapq
import itertools

import jax
import jax.numpy as jnp
from jax import lax
from jax.experimental import pallas as pl
from jax.experimental.pallas import tpu as pltpu
from jax.sharding import PartitionSpec as P

BLK = 128
MAXB = 4
EPS = 1e-05
NS = 8
TX = 4
TZ = 4
NT = TX * TZ
SUB = BLK // NS
NPAIR = 2 * NS
NB = 4
NG = NPAIR - 1 + NB
ROWS = NG * SUB
LANE = 128
NC = 4
WIDTH = LANE * NC * NT
VPART = 1024
NTILE = 1024
DOWN = 2.0 ** -58
UP = 2.0 ** 58
F32 = jnp.float32
MESH = pl.DeviceIdType.MESH
ORDER = (0, 2, 3, 1)
HOP, LAND, GAP, DOT, DEPTH = 1.68, 2.2, 1.3, 0.33, 1


def long_sign(c):
    return 1 if c % 2 == 0 else -1


def rel_of(c, a, b):
    dx, dz = (a, b) if c < NC // 2 else (b, a)
    return (dx % TX) * TZ + dz % TZ


def step_of(c, axis, sign):
    along_x = (axis == 0) == (c < NC // 2)
    return (sign, 0) if along_x else (0, sign)


def forwards(c, a, b):
    go = long_sign(c)
    if (a, b) == (0, 0):
        return [(0, go), (0, -go), (1, go), (1, -go)]
    if b == 0:
        out = [(0, go)] if a == -go else []
        return out + [(1, go), (1, -go)]
    return [(1, go)] if b == -go else []


def wrap(v):
    v = v % 4
    return v - 4 if v == 3 else v


def ahead(c, a, b):
    return max([1 + ahead(c, *moved(a, b, axis, sign)) for axis, sign in forwards(c, a, b)], default=0)


def moved(a, b, axis, sign):
    return (wrap(a - sign), b) if axis == 0 else (a, wrap(b - sign))


def plan():
    tick = itertools.count()
    heap = [(GAP * i, 0, next(tick), ("own", c, 0, 0)) for i, c in enumerate(ORDER)]
    pending, loaded, free, ready = {}, {}, {}, {}
    steps, dots = [], []

    def feed(hop, now):
        queue = pending.get(hop, [])
        while queue and loaded.get(hop, 0) <= DEPTH:
            queue.sort()
            _, _, _, c, a, b, axis, sign = queue.pop(0)
            free[hop] = max(now, free.get(hop, 0.0)) + HOP
            loaded[hop] = loaded.get(hop, 0) + 1
            steps.append(("send", c, a, b, axis, sign))
            heapq.heappush(heap, (free[hop], 2, next(tick), ("free", hop)))
            landed = ("wait", c) + moved(a, b, axis, sign)
            heapq.heappush(heap, (free[hop] + LAND + 0.01 * ORDER.index(c), 1, next(tick), landed))

    now = 0.0
    while heap:
        at, _, _, event = heapq.heappop(heap)
        now = max(now, at)
        if event[0] == "free":
            loaded[event[1]] -= 1
            feed(event[1], at)
            continue
        steps.append(event)
        _, c, a, b = event
        for axis, sign in forwards(c, a, b):
            hop = step_of(c, axis, sign)
            rank = (-ahead(c, *moved(a, b, axis, sign)), -ORDER.index(c), next(tick))
            pending.setdefault(hop, []).append(rank + (c, a, b, axis, sign))
        for axis, sign in forwards(c, a, b):
            feed(step_of(c, axis, sign), now)
        key = (rel_of(c, a, b), c // 2)
        ready[key] = ready.get(key, 0) + 1
        if ready[key] == 2:
            dots.append(("dot",) + key)
        if dots and event[0] == "wait":
            steps.append(dots.pop(0))
            now += DOT
    return steps + dots


STEPS = plan()
FIRST_USE = list(dict.fromkeys(s[1] for s in STEPS if s[0] == "dot"))


FAR_FIRST = sorted(range(1, NT), key=lambda k: -abs(wrap(k // TZ)) - abs(wrap(k % TZ)))


def kernel(
    eb_hbm, ec_hbm, gain_hbm, tgt_hbm, stream_hbm, delta_hbm, w_hbm, out_ref,
    eb_s, ec_s, meta_s, own_s, blk_s, grp_s,
    gain_v, tgt_v, stream_v, delta_v, abuf, hid, sq, gath, wv, acc,
    ss_x, ss_z, scale_v, prob_v, tstat, tcol, pst, stat_v, loss_y, tot_v,
    loc_sem, w_sem, meta_send, meta_recv, a_send, a_recv, g_send, g_recv, ex_send, ex_recv, st_send, st_recv, y_send, y_recv,
):
    sec = lax.axis_index("section")
    tp = lax.axis_index("tp")
    px, pz = tp // TZ, tp % TZ

    def plane(dx, dz):
        return (sec, ((px + dx) % TX) * TZ + (pz + dz) % TZ)

    sec_peers = [((sec + k) % NS, tp) for k in (4, 3, 5, 2, 6, 1, 7)]
    x_peers = [plane(k, 0) for k in range(1, TX)]
    z_peers = [plane(0, k) for k in range(1, TZ)]
    tp_peers = [plane(k // TZ, k % TZ) for k in FAR_FIRST]
    everyone = sec_peers + [plane(1, 0), plane(-1, 0), plane(0, 1), plane(0, -1)]

    barrier = pltpu.get_barrier_semaphore()
    for peer in everyone:
        pl.semaphore_signal(barrier, inc=1, device_id=peer, device_id_type=MESH)

    local = [
        pltpu.make_async_copy(eb_hbm, eb_s, loc_sem.at[0]),
        pltpu.make_async_copy(ec_hbm, ec_s, loc_sem.at[1]),
        pltpu.make_async_copy(stream_hbm.at[:, sec], stream_v, loc_sem.at[2]),
        pltpu.make_async_copy(gain_hbm, gain_v, loc_sem.at[3]),
        pltpu.make_async_copy(tgt_hbm, tgt_v, loc_sem.at[4]),
    ]
    own_delta = [
        pltpu.make_async_copy(
            delta_hbm.at[:, sec, :, pl.ds(c * LANE, LANE)], abuf.at[c, sec], loc_sem.at[5 + c]
        )
        for c in range(NC)
    ]
    all_delta = pltpu.make_async_copy(delta_hbm, delta_v, loc_sem.at[10])
    for copy in local[:2] + [all_delta] + local[2:] + own_delta:
        copy.start()

    local[0].wait()
    local[1].wait()
    for k in range(MAXB):
        meta_s[sec, 0, k] = eb_s[0, k]
    meta_s[sec, 0, MAXB] = ec_s[0, 0]

    all_delta.wait()
    pl.semaphore_wait(barrier, len(everyone))

    sends = []

    def send(src, dst, send_sem, recv_sem, peer):
        copy = pltpu.make_async_remote_copy(
            src_ref=src, dst_ref=dst, send_sem=send_sem, recv_sem=recv_sem,
            device_id=peer, device_id_type=MESH,
        )
        copy.start()
        sends.append(copy)

    def arrived(dst, recv_sem, any_sem):
        pltpu.make_async_remote_copy(
            src_ref=dst, dst_ref=dst, send_sem=any_sem, recv_sem=recv_sem,
            device_id=x_peers[0], device_id_type=MESH,
        ).wait_recv()

    for k, peer in enumerate(sec_peers):
        send(meta_s.at[sec], meta_s.at[sec], meta_send.at[k], meta_recv.at[sec], peer)
    for c in ORDER:
        for k, peer in enumerate(sec_peers):
            send(
                delta_v.at[:, peer[0], :, pl.ds(c * LANE, LANE)], abuf.at[c, sec],
                a_send.at[c, k], a_recv.at[c, sec], peer,
            )

    w_copies = {}
    for i, rel in enumerate(FIRST_USE):
        src_tp = ((px + rel // TZ) % TX) * TZ + (pz + rel % TZ) % TZ
        w_copies[rel] = pltpu.make_async_copy(w_hbm.at[src_tp], wv.at[rel], w_sem.at[i])
        w_copies[rel].start()

    for peer in sec_peers:
        arrived(meta_s.at[peer[0]], meta_recv.at[peer[0]], meta_send.at[0])
    counts = [meta_s[u, 0, MAXB] for u in range(NS)]
    offs = [jnp.int32(0)]
    for u in range(NS - 1):
        offs.append(offs[-1] + counts[u])
    for j in range(NPAIR):
        owner = jnp.int32(0)
        base = jnp.int32(0)
        for u in range(1, NS):
            owner = jnp.where(offs[u] <= j, u, owner)
            base = jnp.where(offs[u] <= j, offs[u], base)
        block = meta_s[owner, 0, jnp.minimum(j - base, MAXB - 1)]
        own_s[j] = owner
        blk_s[j] = block
        grp_s[j] = j if j < NPAIR - 1 else NPAIR - 1 + block

    local[2].wait()
    local[3].wait()
    local[4].wait()

    hop = itertools.count()

    def pass_on(c, a, b, axis, sign):
        there = rel_of(c, *moved(a, b, axis, sign))
        send(
            gath.at[rel_of(c, a, b), c], gath.at[there, c],
            g_send.at[next(hop)], g_recv.at[there, c],
            plane(*step_of(c, axis, sign)),
        )

    def own_shard(c):
        own_delta[c].wait()
        for peer in sec_peers:
            arrived(abuf.at[c, peer[0]], a_recv.at[c, peer[0]], a_send.at[0, 0])
        state = stream_v[:, :, pl.ds(c * LANE, LANE)].astype(F32)
        for u in range(NS):
            state = state + abuf[c, u].astype(F32)
            hid[u] = state
        gain = gain_v[c : c + 1, :] * DOWN

        def put(g, rows):
            sq[g] = rows * rows if c == ORDER[0] else sq[g] + rows * rows
            gath[0, c, pl.ds(g * SUB, SUB), :] = (rows * gain).astype(jnp.bfloat16)

        for j in range(NPAIR - 1):
            put(j, hid[own_s[j], blk_s[j]])
        for b in range(NB):
            put(NPAIR - 1 + b, hid[NS - 1, b])

    def share(buf, place, peers, stage):
        for k, peer in enumerate(peers):
            send(buf.at[place], buf.at[place], ex_send.at[stage, k], ex_recv.at[stage, place], peer)

    def collect(buf, place, stage):
        for k in range(1, 4):
            there = (place + k) % 4
            arrived(buf.at[there], ex_recv.at[stage, there], ex_send.at[stage, 0])

    def squares():
        for g in range(NG, 24):
            sq[g] = jnp.zeros((SUB, LANE), F32)
        sums = []
        for q in range(3):
            part = sq[pl.ds(q * 8, 8)].reshape(LANE, LANE)
            sums.append(jnp.sum(part.T, axis=0, keepdims=True))
        ss_x[px] = jnp.concatenate(sums + [jnp.zeros((5, LANE), F32)], axis=0)
        share(ss_x, px, x_peers, 0)

    lane_r = lax.broadcasted_iota(jnp.int32, (SUB, LANE), 1)

    def columns():
        sub_r = lax.broadcasted_iota(jnp.int32, (SUB, LANE), 0)
        mine = lane_r == sec * SUB + sub_r
        for b in range(NB):
            row = jnp.broadcast_to(tgt_v[b : b + 1, :].astype(F32), (SUB, LANE))
            col = jnp.sum(jnp.where(mine, row, 0.0), axis=1, keepdims=True)
            tcol[b] = jnp.broadcast_to(col, (SUB, LANE)) - (tp * VPART).astype(F32)

    seen = set()
    waits = owns = 0
    for step in STEPS:
        if step[0] == "own":
            own_shard(step[1])
            owns += 1
            first_wait = waits
        elif step[0] == "send":
            pass_on(*step[1:])
        elif step[0] == "wait":
            _, c, a, b = step
            rel = rel_of(c, a, b)
            arrived(gath.at[rel, c], g_recv.at[rel, c], g_send.at[0])
            waits += 1
            if owns == NC and waits == first_wait + 1:
                squares()
                columns()
            if owns == NC and waits == first_wait + 10:
                collect(ss_x, px, 0)
                ss_z[pz] = ss_x[0] + ss_x[1] + ss_x[2] + ss_x[3]
                share(ss_z, pz, z_peers, 1)
            if owns == NC and waits == first_wait + 24:
                collect(ss_z, pz, 1)
                total = ss_z[0] + ss_z[1] + ss_z[2] + ss_z[3]
                scale = lax.rsqrt(total / WIDTH + EPS) * UP
                for q in range(3):
                    wide = jnp.broadcast_to(scale[q : q + 1, :], (LANE, LANE)).T
                    scale_v[pl.ds(q * 8, 8)] = wide.reshape(8, SUB, LANE)
        else:
            _, rel, half = step
            if rel not in seen:
                w_copies[rel].wait()
            first = not seen
            seen.add(rel)

            def tile(n, carry, rel=rel, half=half, first=first):
                cols = pl.ds(pl.multiple_of(n * NTILE, NTILE), NTILE)
                lhs = jnp.concatenate([gath[rel, 2 * half], gath[rel, 2 * half + 1]], axis=1)
                rhs = wv[rel, pl.ds(half * 2 * LANE, 2 * LANE), cols]
                part = jnp.dot(lhs, rhs, preferred_element_type=F32).reshape(NG, SUB, NTILE)
                acc[:, :, cols] = part if first else acc[:, :, cols] + part
                return carry

            lax.fori_loop(0, VPART // NTILE, tile, 0)

    def wide8(v):
        return jnp.concatenate([v] * (VPART // LANE), axis=1)

    def teach(b, carry):
        logit = acc[NPAIR - 1 + b] * wide8(scale_v[NPAIR - 1 + b])
        peak = jnp.max(logit, axis=1, keepdims=True)
        weight = jnp.exp(logit - peak)
        prob_v[b] = weight
        total = jnp.sum(weight, axis=1, keepdims=True)
        tstat[b] = jnp.where(lane_r == 2, peak, jnp.where(lane_r == 3, total, 0.0))
        return carry

    lax.fori_loop(0, NB, teach, 0, unroll=True)
    column = lax.broadcasted_iota(jnp.int32, (SUB, VPART), 1).astype(F32)

    def leave(j, carry):
        block = blk_s[j]
        group = grp_s[j]
        exit_logit = acc[group] * wide8(scale_v[group])
        teach_logit = acc[NPAIR - 1 + block] * wide8(scale_v[NPAIR - 1 + block])
        weight = prob_v[block]
        peak = jnp.max(exit_logit, axis=1, keepdims=True)
        total = jnp.sum(jnp.exp(exit_logit - peak), axis=1, keepdims=True)
        cross = jnp.sum(weight * (teach_logit - exit_logit), axis=1, keepdims=True)
        hit = wide8(tcol[block]) == column
        picked = jnp.sum(jnp.where(hit, exit_logit, 0.0), axis=1, keepdims=True)
        out = tstat[block]
        for k, v in ((0, peak), (1, total), (4, cross), (5, picked)):
            out = jnp.where(lane_r == k, v, out)
        pst[j] = out
        return carry

    lax.fori_loop(0, NPAIR, leave, 0, unroll=True)
    halves = []
    for q in range(2):
        st = pst[pl.ds(q * 8, 8)].reshape(LANE, LANE).T
        lse_e = st[0:1, :] + jnp.log(st[1:2, :])
        lse_t = st[2:3, :] + jnp.log(st[3:4, :])
        halves += [lse_e, lse_t, st[4:5, :] / st[3:4, :], st[5:6, :]]
    stat_v[tp] = jnp.concatenate(halves, axis=0)
    early = list(sends)
    sends.clear()
    for k, (_, there) in enumerate(tp_peers):
        send(stat_v.at[tp], stat_v.at[tp], st_send.at[k], st_recv.at[tp], (sec, there))
    for copy in early:
        copy.wait_send()
    for _, there in tp_peers:
        arrived(stat_v.at[there], st_recv.at[there], st_send.at[0])
    parts = [stat_v[i] for i in range(NT)]
    peak = functools.reduce(jnp.maximum, parts)
    mass = picked = cross = 0.0
    for p in parts:
        share_of = jnp.exp(p - peak)
        mass = mass + share_of
        cross = cross + pltpu.roll(share_of, 1, 0) * p
        picked = picked + p
    lse = peak + jnp.log(mass)
    loss = jnp.concatenate(
        [
            2.0 * lse[q : q + 1] - picked[q + 3 : q + 4] + cross[q + 2 : q + 3] / mass[q + 1 : q + 2] - lse[q + 1 : q + 2]
            for q in (0, 4)
        ],
        axis=1,
    )

    at = lax.broadcasted_iota(jnp.int32, (NPAIR, NPAIR * SUB), 1) // SUB
    pair = lax.broadcasted_iota(jnp.int32, (NPAIR, NPAIR * SUB), 0)
    spread = jnp.where(at == pair, jnp.broadcast_to(loss, (NPAIR, NPAIR * SUB)), 0.0)
    spread = spread[:, :LANE] + spread[:, LANE:]
    for shift in (64, 32, 16):
        spread = spread + pltpu.roll(spread, shift, 1)
    place = lax.broadcasted_iota(jnp.int32, (NPAIR, LANE), 1) // SUB
    low, high = spread[: NPAIR // 2], spread[NPAIR // 2 :]
    place = place[: NPAIR // 2]
    loss_y[sec] = jnp.where(place == 0, low, jnp.where(place == 1, high, 0.0))
    early = list(sends)
    sends.clear()
    for k, peer in enumerate(sec_peers):
        send(loss_y.at[sec], loss_y.at[sec], y_send.at[k], y_recv.at[sec], peer)
    for copy in early:
        copy.wait_send()
    for peer in sec_peers:
        arrived(loss_y.at[peer[0]], y_recv.at[peer[0]], y_send.at[0])
    low = high = jnp.zeros((NPAIR // 2, LANE), F32)
    for u in range(NS):
        low = jnp.where(place == u, pltpu.roll(loss_y[u], SUB * u, 1), low)
        high = jnp.where(place == u, pltpu.roll(loss_y[u], (SUB * (u - 1)) % LANE, 1), high)
    tot_v[pl.ds(0, NPAIR // 2)] = low
    tot_v[pl.ds(NPAIR // 2, NPAIR // 2)] = high
    tot_v[pl.ds(NPAIR, 8)] = jnp.zeros((8, LANE), F32)
    start = jnp.int32(0)
    for u in range(NS):
        start = start + jnp.where(u < sec, counts[u], 0)
    for k in range(MAXB):
        row = tot_v[pl.ds(start + k, 1), :]
        out_ref[0, pl.ds(k, 1), :] = jnp.where(k < ec_s[0, 0], row, 0.0)
    for copy in sends:
        copy.wait_send()


def body(stream_in, layer_delta, norm_gain, out_embed, exit_blocks, exit_counts, targets):
    feat = stream_in.shape[1]
    any_spec = pl.BlockSpec(memory_space=pl.ANY)
    dma = pltpu.SemaphoreType.DMA
    bf16, i32 = jnp.bfloat16, jnp.int32
    vm = pltpu.VMEM
    return pl.pallas_call(
        kernel,
        out_shape=jax.ShapeDtypeStruct((1, MAXB, BLK), F32),
        in_specs=[any_spec] * 7,
        out_specs=pl.BlockSpec(memory_space=pltpu.VMEM),
        scratch_shapes=[
            pltpu.SMEM((1, MAXB), i32),
            pltpu.SMEM((1, 1), i32),
            pltpu.SMEM((NS, 1, LANE), i32),
            pltpu.SMEM((NPAIR,), i32),
            pltpu.SMEM((NPAIR,), i32),
            pltpu.SMEM((NPAIR,), i32),
            vm((NC, LANE), F32),
            vm((NB, BLK), i32),
            vm((NB, SUB, feat), bf16),
            vm((NB, NS, SUB, feat), bf16),
            vm((NC, NS, NB, SUB, LANE), bf16),
            vm((NS, NB, SUB, LANE), F32),
            vm((24, SUB, LANE), F32),
            vm((NT, NC, ROWS, LANE), bf16),
            vm((NT, NC * LANE, VPART), bf16),
            vm((NG, SUB, VPART), F32),
            vm((TX, 8, LANE), F32),
            vm((TZ, 8, LANE), F32),
            vm((24, SUB, LANE), F32),
            vm((NB, SUB, VPART), F32),
            vm((NB, SUB, LANE), F32),
            vm((NB, SUB, LANE), F32),
            vm((NPAIR, SUB, LANE), F32),
            vm((NT, 8, LANE), F32),
            vm((NS, NPAIR // 2, LANE), F32),
            vm((24, LANE), F32),
            dma((11,)),
            dma((NT,)),
            dma((NS - 1,)),
            dma((NS,)),
            dma((NC, NS - 1)),
            dma((NC, NS)),
            dma((NC * (NT - 1),)),
            dma((NT, NC)),
            dma((2, 3)),
            dma((2, 4)),
            dma((NT - 1,)),
            dma((NT,)),
            dma((NS - 1,)),
            dma((NS,)),
        ],
        compiler_params=pltpu.CompilerParams(
            collective_id=0, has_side_effects=True, vmem_limit_bytes=48 * 1024 * 1024
        ),
    )(
        pltpu.with_memory_space_constraint(exit_blocks, pltpu.HBM),
        exit_counts.reshape(1, 1),
        pltpu.with_memory_space_constraint(norm_gain.reshape(NC, LANE), pltpu.HBM),
        pltpu.with_memory_space_constraint(targets.reshape(NB, BLK), pltpu.HBM),
        pltpu.with_memory_space_constraint(stream_in.reshape(NB, NS, SUB, feat), pltpu.HBM),
        pltpu.with_memory_space_constraint(layer_delta.reshape(NB, NS, SUB, feat), pltpu.HBM),
        out_embed.reshape(NT, NC * LANE, VPART),
    )


def solution(mesh):
    placed = (
        P(None, "tp"),
        P("section", None, "tp"),
        P("tp"),
        P(None, "tp"),
        P("section", None),
        P("section"),
        P(),
    )
    return jax.shard_map(
        body, mesh=mesh, in_specs=placed, out_specs=P("section", None, None), check_vma=False
    )
```

```python
import functools
import heapq
import itertools

import jax
import jax.numpy as jnp
from jax import lax
from jax.experimental import pallas as pl
from jax.experimental.pallas import tpu as pltpu
from jax.sharding import PartitionSpec as P

BLK = 128
MAXB = 4
EPS = 1e-05
NS = 8
TX = 4
TZ = 4
NT = TX * TZ
SUB = BLK // NS
NPAIR = 2 * NS
NB = 4
NG = NPAIR - 1 + NB
ROWS = NG * SUB
LANE = 128
NC = 4
WIDTH = LANE * NC * NT
VPART = 1024
NTILE = 1024
DOWN = 2.0 ** -58
UP = 2.0 ** 58
F32 = jnp.float32
MESH = pl.DeviceIdType.MESH
ORDER = (0, 2, 3, 1)
HOP, LAND, GAP, DOT, DEPTH = 1.68, 2.2, 1.3, 0.33, 1


def long_sign(c):
    return 1 if c % 2 == 0 else -1


def rel_of(c, a, b):
    dx, dz = (a, b) if c < NC // 2 else (b, a)
    return (dx % TX) * TZ + dz % TZ


def step_of(c, axis, sign):
    along_x = (axis == 0) == (c < NC // 2)
    return (sign, 0) if along_x else (0, sign)


def forwards(c, a, b):
    go = long_sign(c)
    if (a, b) == (0, 0):
        return [(0, go), (0, -go), (1, go), (1, -go)]
    if b == 0:
        out = [(0, go)] if a == -go else []
        return out + [(1, go), (1, -go)]
    return [(1, go)] if b == -go else []


def wrap(v):
    v = v % 4
    return v - 4 if v == 3 else v


def ahead(c, a, b):
    return max([1 + ahead(c, *moved(a, b, axis, sign)) for axis, sign in forwards(c, a, b)], default=0)


def moved(a, b, axis, sign):
    return (wrap(a - sign), b) if axis == 0 else (a, wrap(b - sign))


def plan():
    tick = itertools.count()
    heap = [(GAP * i, 0, next(tick), ("own", c, 0, 0)) for i, c in enumerate(ORDER)]
    pending, loaded, free, ready = {}, {}, {}, {}
    steps, dots = [], []

    def feed(hop, now):
        queue = pending.get(hop, [])
        while queue and loaded.get(hop, 0) <= DEPTH:
            queue.sort()
            _, _, _, c, a, b, axis, sign = queue.pop(0)
            free[hop] = max(now, free.get(hop, 0.0)) + HOP
            loaded[hop] = loaded.get(hop, 0) + 1
            steps.append(("send", c, a, b, axis, sign))
            heapq.heappush(heap, (free[hop], 2, next(tick), ("free", hop)))
            landed = ("wait", c) + moved(a, b, axis, sign)
            heapq.heappush(heap, (free[hop] + LAND + 0.01 * ORDER.index(c), 1, next(tick), landed))

    now = 0.0
    while heap:
        at, _, _, event = heapq.heappop(heap)
        now = max(now, at)
        if event[0] == "free":
            loaded[event[1]] -= 1
            feed(event[1], at)
            continue
        steps.append(event)
        _, c, a, b = event
        for axis, sign in forwards(c, a, b):
            hop = step_of(c, axis, sign)
            rank = (-ahead(c, *moved(a, b, axis, sign)), -ORDER.index(c), next(tick))
            pending.setdefault(hop, []).append(rank + (c, a, b, axis, sign))
        for axis, sign in forwards(c, a, b):
            feed(step_of(c, axis, sign), now)
        key = (rel_of(c, a, b), c // 2)
        ready[key] = ready.get(key, 0) + 1
        if ready[key] == 2:
            dots.append(("dot",) + key)
        if dots and event[0] == "wait":
            steps.append(dots.pop(0))
            now += DOT
    return steps + dots


STEPS = plan()
FIRST_USE = list(dict.fromkeys(s[1] for s in STEPS if s[0] == "dot"))


FAR_FIRST = sorted(range(1, NT), key=lambda k: -abs(wrap(k // TZ)) - abs(wrap(k % TZ)))


def kernel(
    eb_hbm, ec_hbm, gain_hbm, tgt_hbm, stream_hbm, delta_hbm, w_hbm, out_ref,
    eb_s, ec_s, meta_s, own_s, blk_s, grp_s,
    gain_v, tgt_v, stream_v, delta_v, abuf, hid, sq, gath, wv, acc,
    ss_x, ss_z, scale_v, prob_v, tstat, tcol, pst, stat_v, loss_y, tot_v,
    loc_sem, w_sem, meta_send, meta_recv, a_send, a_recv, g_send, g_recv, ex_send, ex_recv, st_send, st_recv, y_send, y_recv,
):
    sec = lax.axis_index("section")
    tp = lax.axis_index("tp")
    px, pz = tp // TZ, tp % TZ

    def plane(dx, dz):
        return (sec, ((px + dx) % TX) * TZ + (pz + dz) % TZ)

    sec_peers = [((sec + k) % NS, tp) for k in (4, 3, 5, 2, 6, 1, 7)]
    x_peers = [plane(k, 0) for k in range(1, TX)]
    z_peers = [plane(0, k) for k in range(1, TZ)]
    tp_peers = [plane(k // TZ, k % TZ) for k in FAR_FIRST]
    everyone = sec_peers + [plane(1, 0), plane(-1, 0), plane(0, 1), plane(0, -1)]

    barrier = pltpu.get_barrier_semaphore()
    for peer in everyone:
        pl.semaphore_signal(barrier, inc=1, device_id=peer, device_id_type=MESH)

    local = [
        pltpu.make_async_copy(eb_hbm, eb_s, loc_sem.at[0]),
        pltpu.make_async_copy(ec_hbm, ec_s, loc_sem.at[1]),
        pltpu.make_async_copy(stream_hbm.at[:, sec], stream_v, loc_sem.at[2]),
        pltpu.make_async_copy(gain_hbm, gain_v, loc_sem.at[3]),
        pltpu.make_async_copy(tgt_hbm, tgt_v, loc_sem.at[4]),
    ]
    own_delta = [
        pltpu.make_async_copy(
            delta_hbm.at[:, sec, :, pl.ds(c * LANE, LANE)], abuf.at[c, sec], loc_sem.at[5 + c]
        )
        for c in range(NC)
    ]
    all_delta = pltpu.make_async_copy(delta_hbm, delta_v, loc_sem.at[10])
    for copy in local[:2] + [all_delta] + local[2:] + own_delta:
        copy.start()

    local[0].wait()
    local[1].wait()
    for k in range(MAXB):
        meta_s[sec, 0, k] = eb_s[0, k]
    meta_s[sec, 0, MAXB] = ec_s[0, 0]

    all_delta.wait()
    pl.semaphore_wait(barrier, len(everyone))

    sends = []

    def send(src, dst, send_sem, recv_sem, peer):
        copy = pltpu.make_async_remote_copy(
            src_ref=src, dst_ref=dst, send_sem=send_sem, recv_sem=recv_sem,
            device_id=peer, device_id_type=MESH,
        )
        copy.start()
        sends.append(copy)

    def arrived(dst, recv_sem, any_sem):
        pltpu.make_async_remote_copy(
            src_ref=dst, dst_ref=dst, send_sem=any_sem, recv_sem=recv_sem,
            device_id=x_peers[0], device_id_type=MESH,
        ).wait_recv()

    for k, peer in enumerate(sec_peers):
        send(meta_s.at[sec], meta_s.at[sec], meta_send.at[k], meta_recv.at[sec], peer)
    for c in ORDER:
        for k, peer in enumerate(sec_peers):
            send(
                delta_v.at[:, peer[0], :, pl.ds(c * LANE, LANE)], abuf.at[c, sec],
                a_send.at[c, k], a_recv.at[c, sec], peer,
            )

    w_copies = {}
    for i, rel in enumerate(FIRST_USE):
        src_tp = ((px + rel // TZ) % TX) * TZ + (pz + rel % TZ) % TZ
        w_copies[rel] = pltpu.make_async_copy(w_hbm.at[src_tp], wv.at[rel], w_sem.at[i])
        w_copies[rel].start()

    for peer in sec_peers:
        arrived(meta_s.at[peer[0]], meta_recv.at[peer[0]], meta_send.at[0])
    counts = [meta_s[u, 0, MAXB] for u in range(NS)]
    offs = [jnp.int32(0)]
    for u in range(NS - 1):
        offs.append(offs[-1] + counts[u])
    for j in range(NPAIR):
        owner = jnp.int32(0)
        base = jnp.int32(0)
        for u in range(1, NS):
            owner = jnp.where(offs[u] <= j, u, owner)
            base = jnp.where(offs[u] <= j, offs[u], base)
        block = meta_s[owner, 0, jnp.minimum(j - base, MAXB - 1)]
        own_s[j] = owner
        blk_s[j] = block
        grp_s[j] = j if j < NPAIR - 1 else NPAIR - 1 + block

    local[2].wait()
    local[3].wait()
    local[4].wait()

    hop = itertools.count()

    def pass_on(c, a, b, axis, sign):
        there = rel_of(c, *moved(a, b, axis, sign))
        send(
            gath.at[rel_of(c, a, b), c], gath.at[there, c],
            g_send.at[next(hop)], g_recv.at[there, c],
            plane(*step_of(c, axis, sign)),
        )

    def own_shard(c):
        own_delta[c].wait()
        for peer in sec_peers:
            arrived(abuf.at[c, peer[0]], a_recv.at[c, peer[0]], a_send.at[0, 0])
        state = stream_v[:, :, pl.ds(c * LANE, LANE)].astype(F32)
        for u in range(NS):
            state = state + abuf[c, u].astype(F32)
            hid[u] = state
        gain = gain_v[c : c + 1, :] * DOWN

        def put(g, rows):
            sq[g] = rows * rows if c == ORDER[0] else sq[g] + rows * rows
            gath[0, c, pl.ds(g * SUB, SUB), :] = (rows * gain).astype(jnp.bfloat16)

        for j in range(NPAIR - 1):
            put(j, hid[own_s[j], blk_s[j]])
        for b in range(NB):
            put(NPAIR - 1 + b, hid[NS - 1, b])

    def share(buf, place, peers, stage):
        for k, peer in enumerate(peers):
            send(buf.at[place], buf.at[place], ex_send.at[stage, k], ex_recv.at[stage, place], peer)

    def collect(buf, place, stage):
        for k in range(1, 4):
            there = (place + k) % 4
            arrived(buf.at[there], ex_recv.at[stage, there], ex_send.at[stage, 0])

    def squares():
        for g in range(NG, 24):
            sq[g] = jnp.zeros((SUB, LANE), F32)
        sums = []
        for q in range(3):
            part = sq[pl.ds(q * 8, 8)].reshape(LANE, LANE)
            sums.append(jnp.sum(part.T, axis=0, keepdims=True))
        ss_x[px] = jnp.concatenate(sums + [jnp.zeros((5, LANE), F32)], axis=0)
        share(ss_x, px, x_peers, 0)

    lane_r = lax.broadcasted_iota(jnp.int32, (SUB, LANE), 1)

    def columns():
        sub_r = lax.broadcasted_iota(jnp.int32, (SUB, LANE), 0)
        mine = lane_r == sec * SUB + sub_r
        for b in range(NB):
            row = jnp.broadcast_to(tgt_v[b : b + 1, :].astype(F32), (SUB, LANE))
            col = jnp.sum(jnp.where(mine, row, 0.0), axis=1, keepdims=True)
            tcol[b] = jnp.broadcast_to(col, (SUB, LANE)) - (tp * VPART).astype(F32)

    start = jnp.int32(0)
    for u in range(NS):
        start = start + jnp.where(u < sec, counts[u], 0)
    tot_v[pl.ds(NPAIR, 8)] = jnp.zeros((8, LANE), F32)

    seen = set()
    waits = owns = 0
    for step in STEPS:
        if step[0] == "own":
            own_shard(step[1])
            owns += 1
            first_wait = waits
        elif step[0] == "send":
            pass_on(*step[1:])
        elif step[0] == "wait":
            _, c, a, b = step
            rel = rel_of(c, a, b)
            arrived(gath.at[rel, c], g_recv.at[rel, c], g_send.at[0])
            waits += 1
            if owns == NC and waits == first_wait + 1:
                squares()
                columns()
            if owns == NC and waits == first_wait + 10:
                collect(ss_x, px, 0)
                ss_z[pz] = ss_x[0] + ss_x[1] + ss_x[2] + ss_x[3]
                share(ss_z, pz, z_peers, 1)
            if owns == NC and waits == first_wait + 24:
                collect(ss_z, pz, 1)
                total = ss_z[0] + ss_z[1] + ss_z[2] + ss_z[3]
                scale = lax.rsqrt(total / WIDTH + EPS) * UP
                for q in range(3):
                    wide = jnp.broadcast_to(scale[q : q + 1, :], (LANE, LANE)).T
                    scale_v[pl.ds(q * 8, 8)] = wide.reshape(8, SUB, LANE)
        else:
            _, rel, half = step
            if rel not in seen:
                w_copies[rel].wait()
            first = not seen
            seen.add(rel)

            def tile(n, carry, rel=rel, half=half, first=first):
                cols = pl.ds(pl.multiple_of(n * NTILE, NTILE), NTILE)
                lhs = jnp.concatenate([gath[rel, 2 * half], gath[rel, 2 * half + 1]], axis=1)
                rhs = wv[rel, pl.ds(half * 2 * LANE, 2 * LANE), cols]
                part = jnp.dot(lhs, rhs, preferred_element_type=F32).reshape(NG, SUB, NTILE)
                acc[:, :, cols] = part if first else acc[:, :, cols] + part
                return carry

            lax.fori_loop(0, VPART // NTILE, tile, 0)

    def wide8(v):
        return jnp.concatenate([v] * (VPART // LANE), axis=1)

    def teach(b, carry):
        logit = acc[NPAIR - 1 + b] * wide8(scale_v[NPAIR - 1 + b])
        peak = jnp.max(logit, axis=1, keepdims=True)
        weight = jnp.exp(logit - peak)
        prob_v[b] = weight
        total = jnp.sum(weight, axis=1, keepdims=True)
        tstat[b] = jnp.where(lane_r == 2, peak, jnp.where(lane_r == 3, total, 0.0))
        return carry

    lax.fori_loop(0, NB, teach, 0, unroll=True)
    column = lax.broadcasted_iota(jnp.int32, (SUB, VPART), 1).astype(F32)

    def leave(j, carry):
        block = blk_s[j]
        group = grp_s[j]
        exit_logit = acc[group] * wide8(scale_v[group])
        teach_logit = acc[NPAIR - 1 + block] * wide8(scale_v[NPAIR - 1 + block])
        weight = prob_v[block]
        peak = jnp.max(exit_logit, axis=1, keepdims=True)
        total = jnp.sum(jnp.exp(exit_logit - peak), axis=1, keepdims=True)
        cross = jnp.sum(weight * (teach_logit - exit_logit), axis=1, keepdims=True)
        hit = wide8(tcol[block]) == column
        picked = jnp.sum(jnp.where(hit, exit_logit, 0.0), axis=1, keepdims=True)
        out = tstat[block]
        for k, v in ((0, peak), (1, total), (4, cross), (5, picked)):
            out = jnp.where(lane_r == k, v, out)
        pst[j] = out
        return carry

    lax.fori_loop(0, NPAIR, leave, 0, unroll=True)
    halves = []
    for q in range(2):
        st = pst[pl.ds(q * 8, 8)].reshape(LANE, LANE).T
        lse_e = st[0:1, :] + jnp.log(st[1:2, :])
        lse_t = st[2:3, :] + jnp.log(st[3:4, :])
        halves += [lse_e, lse_t, st[4:5, :] / st[3:4, :], st[5:6, :]]
    stat_v[tp] = jnp.concatenate(halves, axis=0)
    early = list(sends)
    sends.clear()
    for k, (_, there) in enumerate(tp_peers):
        send(stat_v.at[tp], stat_v.at[tp], st_send.at[k], st_recv.at[tp], (sec, there))
    for copy in early:
        copy.wait_send()
    for _, there in tp_peers:
        arrived(stat_v.at[there], st_recv.at[there], st_send.at[0])
    parts = [stat_v[i] for i in range(NT)]
    peak = functools.reduce(jnp.maximum, parts)
    mass = picked = cross = 0.0
    for p in parts:
        share_of = jnp.exp(p - peak)
        mass = mass + share_of
        cross = cross + pltpu.roll(share_of, 1, 0) * p
        picked = picked + p
    lse = peak + jnp.log(mass)
    loss = jnp.concatenate(
        [
            2.0 * lse[q : q + 1] - picked[q + 3 : q + 4] + cross[q + 2 : q + 3] / mass[q + 1 : q + 2] - lse[q + 1 : q + 2]
            for q in (0, 4)
        ],
        axis=1,
    )

    at = lax.broadcasted_iota(jnp.int32, (NPAIR, NPAIR * SUB), 1) // SUB
    pair = lax.broadcasted_iota(jnp.int32, (NPAIR, NPAIR * SUB), 0)
    spread = jnp.where(at == pair, jnp.broadcast_to(loss, (NPAIR, NPAIR * SUB)), 0.0)
    spread = spread[:, :LANE] + spread[:, LANE:]
    for shift in (64, 32, 16):
        spread = spread + pltpu.roll(spread, shift, 1)
    place = lax.broadcasted_iota(jnp.int32, (NPAIR, LANE), 1) // SUB
    low, high = spread[: NPAIR // 2], spread[NPAIR // 2 :]
    place = place[: NPAIR // 2]
    loss_y[sec] = jnp.where(place == 0, low, jnp.where(place == 1, high, 0.0))
    early = list(sends)
    sends.clear()
    for k, peer in enumerate(sec_peers):
        send(loss_y.at[sec], loss_y.at[sec], y_send.at[k], y_recv.at[sec], peer)
    for copy in early:
        copy.wait_send()
    for peer in sec_peers:
        arrived(loss_y.at[peer[0]], y_recv.at[peer[0]], y_send.at[0])
    low = high = jnp.zeros((NPAIR // 2, LANE), F32)
    for u in range(NS):
        low = jnp.where(place == u, pltpu.roll(loss_y[u], SUB * u, 1), low)
        high = jnp.where(place == u, pltpu.roll(loss_y[u], (SUB * (u - 1)) % LANE, 1), high)
    tot_v[pl.ds(0, NPAIR // 2)] = low
    tot_v[pl.ds(NPAIR // 2, NPAIR // 2)] = high
    for k in range(MAXB):
        row = tot_v[pl.ds(start + k, 1), :]
        out_ref[0, pl.ds(k, 1), :] = jnp.where(k < ec_s[0, 0], row, 0.0)
    for copy in sends:
        copy.wait_send()


def body(stream_in, layer_delta, norm_gain, out_embed, exit_blocks, exit_counts, targets):
    feat = stream_in.shape[1]
    any_spec = pl.BlockSpec(memory_space=pl.ANY)
    dma = pltpu.SemaphoreType.DMA
    bf16, i32 = jnp.bfloat16, jnp.int32
    vm = pltpu.VMEM
    return pl.pallas_call(
        kernel,
        out_shape=jax.ShapeDtypeStruct((1, MAXB, BLK), F32),
        in_specs=[any_spec] * 7,
        out_specs=pl.BlockSpec(memory_space=pltpu.VMEM),
        scratch_shapes=[
            pltpu.SMEM((1, MAXB), i32),
            pltpu.SMEM((1, 1), i32),
            pltpu.SMEM((NS, 1, LANE), i32),
            pltpu.SMEM((NPAIR,), i32),
            pltpu.SMEM((NPAIR,), i32),
            pltpu.SMEM((NPAIR,), i32),
            vm((NC, LANE), F32),
            vm((NB, BLK), i32),
            vm((NB, SUB, feat), bf16),
            vm((NB, NS, SUB, feat), bf16),
            vm((NC, NS, NB, SUB, LANE), bf16),
            vm((NS, NB, SUB, LANE), F32),
            vm((24, SUB, LANE), F32),
            vm((NT, NC, ROWS, LANE), bf16),
            vm((NT, NC * LANE, VPART), bf16),
            vm((NG, SUB, VPART), F32),
            vm((TX, 8, LANE), F32),
            vm((TZ, 8, LANE), F32),
            vm((24, SUB, LANE), F32),
            vm((NB, SUB, VPART), F32),
            vm((NB, SUB, LANE), F32),
            vm((NB, SUB, LANE), F32),
            vm((NPAIR, SUB, LANE), F32),
            vm((NT, 8, LANE), F32),
            vm((NS, NPAIR // 2, LANE), F32),
            vm((24, LANE), F32),
            dma((11,)),
            dma((NT,)),
            dma((NS - 1,)),
            dma((NS,)),
            dma((NC, NS - 1)),
            dma((NC, NS)),
            dma((NC * (NT - 1),)),
            dma((NT, NC)),
            dma((2, 3)),
            dma((2, 4)),
            dma((NT - 1,)),
            dma((NT,)),
            dma((NS - 1,)),
            dma((NS,)),
        ],
        compiler_params=pltpu.CompilerParams(
            collective_id=0, has_side_effects=True, vmem_limit_bytes=48 * 1024 * 1024
        ),
    )(
        pltpu.with_memory_space_constraint(exit_blocks, pltpu.HBM),
        exit_counts.reshape(1, 1),
        pltpu.with_memory_space_constraint(norm_gain.reshape(NC, LANE), pltpu.HBM),
        pltpu.with_memory_space_constraint(targets.reshape(NB, BLK), pltpu.HBM),
        pltpu.with_memory_space_constraint(stream_in.reshape(NB, NS, SUB, feat), pltpu.HBM),
        pltpu.with_memory_space_constraint(layer_delta.reshape(NB, NS, SUB, feat), pltpu.HBM),
        out_embed.reshape(NT, NC * LANE, VPART),
    )


def solution(mesh):
    placed = (
        P(None, "tp"),
        P("section", None, "tp"),
        P("tp"),
        P(None, "tp"),
        P("section", None),
        P("section"),
        P(),
    )
    return jax.shard_map(
        body, mesh=mesh, in_specs=placed, out_specs=P("section", None, None), check_vma=False
    )
```
